768 devices in a mesh: dom: 12 (over z), grp: 64 (over y, x, core).
Axes of the slice: x: 4, y: 8, z: 12, core: 2. Of those that a mesh axis runs over, the one named last changes fastest.
Arguments:
- support: float32 [16, 16, 16, 98304], P(None, None, None, ('dom', 'grp')), may hold values from -6 to 6
- potential: float32 [16, 16, 16, 98304], P(None, None, None, ('dom', 'grp')), may hold values from -6 to 6
- magic_taps: float32 [16], replicated, may hold values from -1 to 1
- kinetic_taps: float32 [16], replicated, may hold values from -1 to 1
- kernel_diag: float32 [98304], P(('dom', 'grp')), may hold values from 0.2 to 5
- owners: int32 [98304, 1], P(('dom', 'grp')), may hold values from 0 to 63; in each aligned block of 128 rows (0 to 127, 128 to 255, ...) at most 3 rows name the same one
Outputs:
- margin: float32 [98304, 128], P(('dom', 'grp'))
- density: float32 [96, 256], P('dom')
The draws below stay inside these ranges and needn't reach their ends.
Inputs may be any that keep to these rules, and one draw needn't show every extreme that they name: `owners`: within each device's aligned block of 128 functions, no owner is named by more than 3 functions, a bound that some block reaches.
All inputs are finite; a program needn't handle non-finite values.
Results may differ from the reference program's by a relative error of at most 0.004.
Values may be sent and summed in bfloat16 or wider, within the bound.
No kernel may reach another device: no remote copies, remote signals or barrier semaphores. Data moves between devices by JAX's collectives and lax.ppermute only.
A program may use at most 32 MiB of HBM per device.

```python
import math
import jax
import jax.numpy as jnp
import numpy as np
from jax import lax

BOX = 16
TAPS = 16
FDEV = 128
CAP = 3
NF = 98304
N_DOM = 12
N_GRP = 64


def levels(own_key, extent, cuts, smallest, high):
    loudness, own = 1.0, jax.random.fold_in(own_key, 6)
    for axis_at, blocks in cuts:
        steps = jnp.exp(jax.random.uniform(jax.random.fold_in(own, axis_at), (blocks,), jnp.float32, smallest / len(cuts), high / len(cuts)))
        loudness = loudness * jnp.repeat(steps, extent[axis_at] // blocks).reshape([-1 if axis == axis_at else 1 for axis in range(len(extent))])
    return loudness


def assign_block(own_key, own, number, rows, count, top, bound, slope):
    sequence = jax.random.permutation(own_key, count)
    packed, common = load_shares(count, rows * top, bound, slope, True), load_shares(count, rows * top, bound, slope, False)
    places = jnp.arange(count)

    def named(lengths, rotation):
        used = int((lengths > 0).sum())
        fixed = max(1, used // 4)
        moved = fixed + (places - fixed + rotation * (used - fixed)) % max(1, count - fixed)
        return jnp.zeros((count,), jnp.int32).at[sequence[jnp.where(places < fixed, places, moved)]].set(jnp.asarray(lengths, jnp.int32))

    lengths = jnp.where(number % 4 == 0, named(packed, number // 4), named(common, number - number // 4 - 1))
    mixed = jax.random.permutation(jax.random.fold_in(own, 3), count)
    donor, taker = mixed[0:count // 2 * 2:2], mixed[1:count // 2 * 2:2]
    room = jnp.minimum(lengths[donor] - 1, bound - lengths[taker]) // 2
    room = jnp.where((donor == sequence[0]) | (taker == sequence[0]) | (lengths[taker] == 0), 0, jnp.maximum(room, 0))
    moved = jax.random.randint(jax.random.fold_in(own, 4), (count // 2,), 0, 1 << 20) % (room + 1)
    lengths = lengths.at[donor].add(-moved).at[taker].add(moved)
    labels = jnp.searchsorted(jnp.cumsum(lengths), jnp.arange(rows * top), side="right").astype(jnp.int32)
    table = labels.reshape(top, rows).T
    table = table[jax.random.permutation(jax.random.fold_in(own, 1), rows)]
    rotation = jax.random.randint(jax.random.fold_in(own, 2), (rows, 1), 0, top)
    return jnp.take_along_axis(table, (jnp.arange(top)[None, :] + rotation) % top, axis=1)


def load_shares(number_of, total, bound, slope, full):
    portions = [(1 << 20) // math.isqrt(rank ** slope) + 1 for rank in range(1, number_of + 1)]
    largest = bound if full else min(bound, max(-(-total // number_of), total * portions[0] // sum(portions)))
    least = 1 if total - largest >= number_of - 1 else 0
    holding, spare = [largest] + [least] * (number_of - 1), total - largest - least * (number_of - 1)
    while spare > 0:
        movable = [i for i in range(1, number_of) if holding[i] < largest] or [i for i in range(1, number_of) if holding[i] < bound]
        mass, remaining = sum([portions[i] for i in movable]), spare
        for i in movable:
            extra = min(bound - holding[i], max(1, remaining * portions[i] // mass), spare)
            holding[i] = holding[i] + extra
            spare = spare - extra
    return np.array(holding)


def bell_draw(own_key, extent, spread, reach, shards=(), kind=jnp.bfloat16):
    entries = spread * jax.random.normal(own_key, extent, jnp.float32)
    if shards:
        entries = entries * levels(own_key, extent, shards, -0.22, 0.18)
    return jnp.clip(entries, -reach, reach).astype(kind)


def setup_inputs(seed: int = 0) -> dict:
    keys = jax.random.split(jax.random.key(seed), 7)
    support = bell_draw(keys[0], (BOX, BOX, BOX, NF), 1.0, 6.0, ((3, 768),), jnp.float32)
    potential = bell_draw(keys[1], (BOX, BOX, BOX, NF), 1.0, 6.0, ((3, 768),), jnp.float32)
    magic_taps = bell_draw(keys[2], (TAPS,), 0.25, 1.0, (), jnp.float32)
    kinetic_taps = bell_draw(keys[3], (TAPS,), 0.25, 1.0, (), jnp.float32)
    kernel_diag = jnp.clip(jnp.exp(math.log(5.0) - 3.218876 * jax.random.uniform(keys[4], (NF,), jnp.float32) ** levels(keys[4], (NF,), ((0, 768),), -0.2, 0.2)), 0.2, 5.0)
    owners_keys = jax.random.split(jax.random.fold_in(keys[5], 1), NF // FDEV)
    owners_turns = jax.random.permutation(jax.random.fold_in(keys[5], 3), NF // FDEV)
    owners = jax.vmap(lambda own, number: assign_block(jax.random.fold_in(keys[5], 2), own, number, FDEV, N_GRP, 1, CAP, 2))(owners_keys, owners_turns).reshape((NF, 1))
    return dict(support=support, potential=potential, magic_taps=magic_taps, kinetic_taps=kinetic_taps, kernel_diag=kernel_diag, owners=owners)


HIGHEST = lax.Precision.HIGHEST


def band_matrix(tap_values, box_side):
    row_index = jnp.arange(box_side)[:, None]
    col_index = jnp.arange(box_side)[None, :]
    offset = col_index - row_index + (tap_values.shape[0] // 2 - 1)
    tap_table = (offset[:, :, None] == jnp.arange(tap_values.shape[0])[None, None, :]).astype(jnp.float32)
    return jnp.einsum("abt,t->ab", tap_table, tap_values, precision=HIGHEST)


def filter_along(matrix, field_block, direction):
    if direction == 0:
        return jnp.einsum("ab,bjkf->ajkf", matrix, field_block, precision=HIGHEST)
    if direction == 1:
        return jnp.einsum("ab,ibkf->iakf", matrix, field_block, precision=HIGHEST)
    return jnp.einsum("ab,ijbf->ijaf", matrix, field_block, precision=HIGHEST)


def apply_block(support, potential, magic_taps, kinetic_taps, kernel_diag):
    box_side = support.shape[0]
    magic_band = band_matrix(magic_taps, box_side)
    kinetic_band = band_matrix(kinetic_taps, box_side)
    realspace = filter_along(magic_band, filter_along(magic_band, filter_along(magic_band, support, 0), 1), 2)
    density_part = jnp.sum(kernel_diag * realspace * realspace, axis=3)
    weighted = potential * realspace
    magic_back = magic_band.T
    returned = filter_along(magic_back, filter_along(magic_back, filter_along(magic_back, weighted, 0), 1), 2)
    kinetic_part = filter_along(kinetic_band, support, 0) + filter_along(kinetic_band, support, 1) + filter_along(kinetic_band, support, 2)
    gradient = (returned + kinetic_part).astype(jnp.bfloat16)
    return gradient, density_part


def reference(support, potential, magic_taps, kinetic_taps, kernel_diag, owners):
    box_side = support.shape[0]
    cell_count = box_side ** 3
    device_count = N_DOM * N_GRP
    scale_factor = 1.0 / float(box_side) ** 1.5

    def block(block_index):
        first_column = block_index * FDEV
        coeff_block = lax.dynamic_slice_in_dim(support, first_column, FDEV, 3)
        field_block = lax.dynamic_slice_in_dim(potential, first_column, FDEV, 3)
        kernel_block = lax.dynamic_slice_in_dim(kernel_diag, first_column, FDEV, 0)
        gradient, density_part = apply_block(coeff_block, field_block, magic_taps, kinetic_taps, kernel_block)
        return gradient.reshape(cell_count, FDEV), density_part / (FDEV * N_GRP)

    gradients, densities = lax.map(block, jnp.arange(device_count, dtype=jnp.int32))
    coeffs = support.reshape(cell_count, device_count, FDEV).astype(jnp.bfloat16)
    kernel_blocks = kernel_diag.reshape(device_count, FDEV)
    owner_blocks = owners.reshape(device_count, FDEV).astype(jnp.int32)

    def rows(block_index):
        domain = block_index // N_GRP
        target = (domain * N_GRP + owner_blocks[block_index]).astype(jnp.int32)
        operands = jnp.take(coeffs, target, axis=1).astype(jnp.float32)
        gradient = gradients[block_index].astype(jnp.float32)
        products = jnp.einsum("ci,cij->ij", gradient, operands, precision=HIGHEST)
        return products * jnp.take(kernel_blocks, target, axis=0) * scale_factor

    margin = lax.map(rows, jnp.arange(device_count, dtype=jnp.int32)).reshape(device_count * FDEV, FDEV)
    boxdens = jnp.sum(densities.reshape(N_DOM, N_GRP, box_side, box_side * box_side), axis=1)
    half_side = box_side // 2
    density = boxdens[:, :half_side] + jnp.roll(boxdens[:, half_side:], 1, axis=0)
    return margin, density.reshape(N_DOM * half_side, box_side * box_side)
```

```python
import functools

import jax
import jax.numpy as jnp
from jax import lax
from jax.experimental import pallas as pl
from jax.experimental.pallas import tpu as pltpu
from jax.sharding import PartitionSpec as P

F32 = jnp.float32
BF16 = jnp.bfloat16
SIDE = 16
PLANE = SIDE * SIDE
CELLS = SIDE**3
LANES = 128
CAP = 3
CHUNKS = CELLS // LANES


def split2(x):
    hi = x.astype(BF16)
    lo = (x - hi.astype(F32)).astype(BF16)
    return hi, lo


def tap_lookup(taps_ref, offset):
    out = jnp.zeros(offset.shape, F32)
    for q in range(SIDE):
        out = jnp.where(offset == q, taps_ref[q], out)
    return out


def store_split(dst, row0, mat):
    hi, lo = split2(mat)
    rows = mat.shape[0]
    dst[pl.ds(row0, rows), 0:PLANE] = hi
    dst[pl.ds(row0, rows), PLANE : 2 * PLANE] = lo
    dst[pl.ds(row0, rows), 2 * PLANE : 3 * PLANE] = hi


def stack3(x):
    hi, lo = split2(x)
    return jnp.concatenate([hi, hi, lo], axis=0)


def mm(a, b):
    return jnp.dot(a, b, preferred_element_type=F32)


def slot_of(owner_row):
    n = owner_row.shape[1]
    across = jnp.broadcast_to(owner_row.astype(F32), (n, n))
    down = across.T
    r = lax.broadcasted_iota(jnp.int32, (n, n), 0)
    c = lax.broadcasted_iota(jnp.int32, (n, n), 1)
    earlier = jnp.where((across == down) & (r < c), 1.0, 0.0)
    return jnp.sum(earlier, axis=0, keepdims=True).astype(jnp.int32)


def apply_kernel(
    groups,
    magic_ref, kinetic_ref, diag_ref, owner_ref, x_hbm, pot_hbm,
    out_ref, dens_ref,
    x_ref, pot_ref, z_ref, kin_ref, v_ref, lhs1, lhs_f, lhs_ft, lhs_k, lhs_b, sel_ref, rows_ref,
    sem_x, sem_p,
):
    copies_x, copies_p = [], []
    for q in range(4):
        part = pl.ds(q * 4, 4)
        copies_x.append(pltpu.make_async_copy(x_hbm.at[part], x_ref.at[part], sem_x.at[q]))
        copies_p.append(pltpu.make_async_copy(pot_hbm.at[part], pot_ref.at[part], sem_p.at[q]))
    for c in copies_x:
        c.start()
    for c in copies_p:
        c.start()

    half = SIDE // 2 - 1
    rr = lax.broadcasted_iota(jnp.int32, (PLANE, PLANE), 0)
    cc = lax.broadcasted_iota(jnp.int32, (PLANE, PLANE), 1)
    d_minor = lax.rem(cc, SIDE) - lax.rem(rr, SIDE)
    d_major = cc // SIDE - rr // SIDE
    same_minor = d_minor == 0
    same_major = d_major == 0
    f_minor = tap_lookup(magic_ref, d_minor + half)
    f_major = tap_lookup(magic_ref, d_major + half)
    k_minor = tap_lookup(kinetic_ref, d_minor + half)
    k_major = tap_lookup(kinetic_ref, d_major + half)
    ft_minor = tap_lookup(magic_ref, half - d_minor)
    ft_major = tap_lookup(magic_ref, half - d_major)
    store_split(lhs1, 0, f_major * f_minor)
    store_split(lhs1, PLANE, jnp.where(same_minor, k_major, 0.0) + jnp.where(same_major, k_minor, 0.0))
    store_split(lhs_f, 0, jnp.where(same_minor, f_major, 0.0))
    store_split(lhs_ft, 0, jnp.where(same_minor, ft_major, 0.0))
    store_split(lhs_k, 0, jnp.where(same_minor, k_major, 0.0))
    store_split(lhs_b, 0, ft_major * ft_minor)

    owner = owner_ref[...]
    column = slot_of(owner) * groups + owner
    ri = lax.broadcasted_iota(jnp.int32, (CAP * groups, LANES), 0)
    sel_ref[...] = jnp.where(ri == column, 1.0, 0.0).astype(BF16)

    def pair(ref, axis, p):
        if axis == 0:
            a, b = ref[2 * p], ref[2 * p + 1]
        else:
            a, b = ref[:, 2 * p], ref[:, 2 * p + 1]
        return jnp.concatenate([a.reshape(PLANE, LANES), b.reshape(PLANE, LANES)], axis=1)

    def halves(y):
        return [y[:, h * LANES : (h + 1) * LANES].reshape(SIDE, SIDE, LANES) for h in (0, 1)]

    for c in copies_x:
        c.wait()

    def phase_a(p, carry):
        y = mm(lhs1[...], stack3(pair(x_ref, 0, p)))
        for h, (z, k) in enumerate(zip(halves(y[:PLANE]), halves(y[PLANE:]))):
            z_ref[2 * p + h] = z
            kin_ref[2 * p + h] = k
        return carry

    lax.fori_loop(0, SIDE // 2, phase_a, 0)
    for c in copies_p:
        c.wait()

    def phase_b(p, carry):
        r = mm(lhs_f[...], stack3(pair(z_ref, 1, p)))
        w = r * pair(pot_ref, 1, p)
        v = mm(lhs_ft[...], stack3(w))
        k = mm(lhs_k[...], stack3(pair(x_ref, 1, p)))
        for h, (rh, vh, kh) in enumerate(zip(halves(r), halves(v), halves(k))):
            z_ref[:, 2 * p + h] = rh
            v_ref[:, 2 * p + h] = vh
            kin_ref[:, 2 * p + h] += kh
        return carry

    lax.fori_loop(0, SIDE // 2, phase_b, 0)

    diag = diag_ref[...] * (1.0 / (LANES * groups))
    ones = jnp.ones((8, 2 * LANES), BF16)
    nt = (((1,), (1,)), ((), ()))

    def phase_c(p, carry):
        g = mm(lhs_b[...], stack3(pair(v_ref, 0, p))) + pair(kin_ref, 0, p)
        gb = g.astype(BF16)
        for h in (0, 1):
            i = 2 * p + h
            r = z_ref[i].reshape(PLANE, LANES)
            hi, lo = split2(diag * r * r)
            d = lax.dot_general(ones, jnp.concatenate([hi, lo], axis=1), nt, preferred_element_type=F32)
            dens_ref[pl.ds(i, 1), :] = d[0:1]
            sent = lax.dot_general(
                sel_ref[...], gb[:, h * LANES : (h + 1) * LANES], nt, preferred_element_type=F32
            )
            for s in range(CAP):
                for c in (0, 1):
                    rows_ref[pl.ds(s * CHUNKS + 2 * i + c, groups, stride=CAP * CHUNKS), :] = sent[
                        s * groups : (s + 1) * groups, c * LANES : (c + 1) * LANES
                    ]
        return carry

    lax.fori_loop(0, SIDE // 2, phase_c, 0)

    def pack(g, carry):
        out_ref[g] = rows_ref[pl.ds(g * CAP * CHUNKS, CAP * CHUNKS), :].astype(BF16)
        return carry

    lax.fori_loop(0, groups, pack, 0, unroll=4)


def run_apply(support, potential, magic_taps, kinetic_taps, kernel_diag, owners, groups):
    vm = pl.BlockSpec(memory_space=pltpu.VMEM)
    sm = pl.BlockSpec(memory_space=pltpu.SMEM)
    hbm = pl.BlockSpec(memory_space=pl.ANY)
    box = (SIDE, SIDE, SIDE, LANES)
    lhs = pltpu.VMEM((PLANE, 3 * PLANE), BF16)

    return pl.pallas_call(
        functools.partial(apply_kernel, groups),
        out_shape=(
            jax.ShapeDtypeStruct((groups, CAP * CHUNKS, LANES), BF16),
            jax.ShapeDtypeStruct((SIDE, PLANE), F32),
        ),
        in_specs=[sm, sm, vm, vm, hbm, hbm],
        out_specs=(vm, vm),
        scratch_shapes=[
            pltpu.VMEM(box, F32), pltpu.VMEM(box, F32), pltpu.VMEM(box, F32), pltpu.VMEM(box, F32), pltpu.VMEM(box, F32),
            pltpu.VMEM((2 * PLANE, 3 * PLANE), BF16), lhs, lhs, lhs, lhs,
            pltpu.VMEM((CAP * groups, LANES), BF16),
            pltpu.VMEM((groups * CAP * CHUNKS, LANES), F32),
            pltpu.SemaphoreType.DMA((4,)), pltpu.SemaphoreType.DMA((4,)),
        ],
        compiler_params=pltpu.CompilerParams(vmem_limit_bytes=48 * 1024 * 1024),
    )(magic_taps, kinetic_taps, kernel_diag.reshape(1, LANES), owners.reshape(1, LANES), support, potential)


def margin_kernel(groups, recv_ref, coef_ref, scale_ref, out_ref, rows_ref):
    def unpack(g, carry):
        rows_ref[pl.ds(g * CAP * CHUNKS, CAP * CHUNKS), :] = recv_ref[g].astype(F32)
        return carry

    lax.fori_loop(0, groups, unpack, 0, unroll=4)

    def step(i, acc):
        parts = []
        for s in range(CAP):
            cols = [
                rows_ref[pl.ds(s * CHUNKS + 2 * i + c, groups, stride=CAP * CHUNKS), :] for c in (0, 1)
            ]
            parts.append(jnp.concatenate(cols, axis=1))
        lhs = jnp.concatenate(parts, axis=0).astype(BF16)
        rhs = coef_ref[pl.ds(pl.multiple_of(i * PLANE, PLANE), PLANE), :].astype(BF16)
        return acc + mm(lhs, rhs)

    acc = lax.fori_loop(0, SIDE, step, jnp.zeros((CAP * groups, LANES), F32))
    acc = acc * (scale_ref[...] * (1.0 / float(SIDE) ** 1.5))
    for s in range(CAP):
        out_ref[pl.ds(s, groups, stride=4), :] = acc[s * groups : (s + 1) * groups]
    out_ref[pl.ds(CAP, groups, stride=4), :] = jnp.zeros((groups, LANES), F32)


def run_margin(received, owned, kernel_diag, groups):

    vm = pl.BlockSpec(memory_space=pltpu.VMEM)
    return pl.pallas_call(
        functools.partial(margin_kernel, groups),
        out_shape=jax.ShapeDtypeStruct((groups * 4, LANES), F32),
        in_specs=[vm, vm, vm],
        out_specs=vm,
        scratch_shapes=[pltpu.VMEM((groups * CAP * CHUNKS, LANES), F32)],
        compiler_params=pltpu.CompilerParams(vmem_limit_bytes=32 * 1024 * 1024),
    )(received, owned, kernel_diag.reshape(1, LANES))


def gather_kernel(owner_ref, ret_ref, out_ref):
    owner = owner_ref[...]
    column = owner * 4 + slot_of(owner)
    n = ret_ref.shape[0]
    ri = lax.broadcasted_iota(jnp.int32, (n, LANES), 0)
    onehot = jnp.where(ri == column, 1.0, 0.0).T.astype(BF16)
    x = ret_ref[...]
    hi, mid = split2(x)
    lo = (x - hi.astype(F32) - mid.astype(F32)).astype(BF16)
    out_ref[...] = mm(onehot, hi) + (mm(onehot, mid) + mm(onehot, lo))


def run_gather(owners, returned):
    vm = pl.BlockSpec(memory_space=pltpu.VMEM)
    return pl.pallas_call(
        gather_kernel,
        out_shape=jax.ShapeDtypeStruct((LANES, LANES), F32),
        in_specs=[vm, vm],
        out_specs=vm,
    )(owners.reshape(1, LANES), returned)


def body(support, potential, magic_taps, kinetic_taps, kernel_diag, owners):
    groups = lax.axis_size("grp")
    domains = lax.axis_size("dom")
    outgoing, part = run_apply(support, potential, magic_taps, kinetic_taps, kernel_diag, owners, groups)
    received = lax.all_to_all(outgoing, "grp", split_axis=0, concat_axis=0, tiled=True)
    distance = 1
    while distance < groups:
        part = part + lax.ppermute(part, "grp", [(i, i ^ distance) for i in range(groups)])
        distance *= 2
    half = SIDE // 2
    upper = lax.ppermute(part[half:], "dom", [(i, (i + 1) % domains) for i in range(domains)])
    density = part[:half] + upper
    products = run_margin(received, support.reshape(CELLS, LANES), kernel_diag, groups)
    returned = lax.all_to_all(
        products.reshape(groups, 4, LANES), "grp", split_axis=0, concat_axis=0, tiled=True
    )
    margin = run_gather(owners, returned.reshape(groups * 4, LANES))
    return margin, density


def solution(mesh):
    return jax.shard_map(
        body,
        mesh=mesh,
        in_specs=(
            P(None, None, None, ("dom", "grp")),
            P(None, None, None, ("dom", "grp")),
            P(),
            P(),
            P(("dom", "grp")),
            P(("dom", "grp"), None),
        ),
        out_specs=(P(("dom", "grp"), None), P("dom", None)),
        check_vma=False,
    )
```

```python
import functools

import jax
import jax.numpy as jnp
from jax import lax
from jax.experimental import pallas as pl
from jax.experimental.pallas import tpu as pltpu
from jax.sharding import PartitionSpec as P

F32 = jnp.float32
BF16 = jnp.bfloat16
SIDE = 16
HALF = SIDE // 2
PLANE = SIDE * SIDE
CELLS = SIDE**3
LANES = 128
CAP = 3
CHUNKS = CELLS // LANES
BLOCK = CAP * CHUNKS
BACK = 8
NT = (((1,), (1,)), ((), ()))

VM = pl.BlockSpec(memory_space=pltpu.VMEM)
HBM = pl.BlockSpec(memory_space=pltpu.HBM)


def split2(x):
    hi = x.astype(BF16)
    lo = (x - hi.astype(F32)).astype(BF16)
    return hi, lo


def mm(a, b):
    return jnp.dot(a, b, preferred_element_type=F32)


def tap_lookup(taps_ref, offset):
    out = jnp.zeros(offset.shape, F32)
    for q in range(SIDE):
        out = jnp.where(offset == q, taps_ref[q], out)
    return out


def stack3(x):
    hi, lo = split2(x)
    return jnp.concatenate([hi, hi, lo], axis=0)


def slot_of(owner_row):
    n = owner_row.shape[1]
    across = jnp.broadcast_to(owner_row.astype(F32), (n, n))
    down = across.T
    r = lax.broadcasted_iota(jnp.int32, (n, n), 0)
    c = lax.broadcasted_iota(jnp.int32, (n, n), 1)
    earlier = jnp.where((across == down) & (r < c), 1.0, 0.0)
    return jnp.sum(earlier, axis=0, keepdims=True).astype(jnp.int32)


def build_plane_matrices(magic, kinetic, pat_ref, lhs1, lhs_b):
    half = SIDE // 2 - 1
    a = lax.broadcasted_iota(jnp.int32, (SIDE, PLANE), 0)
    c = lax.broadcasted_iota(jnp.int32, (SIDE, PLANE), 1)
    minor = jnp.bitwise_and(c, SIDE - 1) - a
    major = jnp.right_shift(c, 4) - a
    f_minor = tap_lookup(magic, minor + half)
    k_minor = tap_lookup(kinetic, minor + half)
    ft_minor = tap_lookup(magic, half - minor)
    pat_ref[0] = tap_lookup(magic, major + half)
    pat_ref[1] = tap_lookup(kinetic, major + half)
    pat_ref[2] = tap_lookup(magic, half - major)
    same_minor = minor == 0
    lane_major = jnp.right_shift(c, 4)

    def put(dst, row, mat, third):
        hi, lo = split2(mat)
        dst[pl.ds(row, SIDE), 0:PLANE] = hi
        dst[pl.ds(row, SIDE), PLANE : 2 * PLANE] = lo
        if third:
            dst[pl.ds(row, SIDE), 2 * PLANE : 3 * PLANE] = hi

    def rows(g, carry):
        r = pl.multiple_of(g * SIDE, SIDE)
        fm = pat_ref[0, pl.ds(g, 1), :]
        km = pat_ref[1, pl.ds(g, 1), :]
        bm = pat_ref[2, pl.ds(g, 1), :]
        put(lhs1, r, fm * f_minor, False)
        put(lhs1, r + PLANE, jnp.where(same_minor, km, 0.0) + jnp.where(lane_major == g, k_minor, 0.0), False)
        put(lhs_b, r, bm * ft_minor, True)
        return carry

    lax.fori_loop(0, SIDE, rows, 0)


def build_side_matrix(taps, lhs, transposed, double):
    n = SIDE * HALF
    half = SIDE // 2 - 1
    r = lax.broadcasted_iota(jnp.int32, (n, n), 0)
    c = lax.broadcasted_iota(jnp.int32, (n, n), 1)
    delta = jnp.right_shift(c, 3) - jnp.right_shift(r, 3)
    offset = half - delta if transposed else delta + half
    same = jnp.bitwise_and(r, HALF - 1) == jnp.bitwise_and(c, HALF - 1)
    hi, lo = split2(tap_lookup(taps, jnp.where(same, offset, -1)))
    lhs[0:n, 0:n] = hi
    if not double:
        lhs[0:n, n : 2 * n] = lo
        return
    lhs[0:n, n : 2 * n] = hi
    lhs[n : 2 * n, 0:n] = lo
    lhs[n : 2 * n, n : 2 * n] = lo


def apply_kernel(
    groups,
    magic_hbm, kinetic_hbm, diag_hbm, owner_hbm, x_hbm, pot_hbm,
    out_hbm, dens_ref,
    x_ref, pot_ref, z_ref, kin_ref, v_ref,
    pat_ref, lhs1, lhs_b, lhs_f, lhs_ft, lhs_k, sel_ref, rows_ref, acc_ref, stage_ref, grad_ref,
    magic, kinetic, diag_ref, owner_ref,
    sem_s, sem_x, sem_p, sem_o,
):
    small = [
        pltpu.make_async_copy(src, dst, sem_s.at[q])
        for q, (src, dst) in enumerate(
            [(magic_hbm, magic), (kinetic_hbm, kinetic), (diag_hbm, diag_ref), (owner_hbm, owner_ref)]
        )
    ]
    parts = 4
    width = SIDE // parts
    copies_x, copies_p = [], []
    for q in range(parts):
        part = pl.ds(q * width, width)
        copies_x.append(pltpu.make_async_copy(x_hbm.at[part], x_ref.at[part], sem_x.at[q]))
        copies_p.append(pltpu.make_async_copy(pot_hbm.at[part], pot_ref.at[part], sem_p.at[q]))
    for c in small + copies_x + copies_p:
        c.start()
    for c in small:
        c.wait()

    build_plane_matrices(magic, kinetic, pat_ref, lhs1, lhs_b)
    build_side_matrix(magic, lhs_f, False, True)
    build_side_matrix(magic, lhs_ft, True, True)
    build_side_matrix(kinetic, lhs_k, False, False)
    owner = owner_ref[...]
    column = slot_of(owner) * groups + owner
    ri = lax.broadcasted_iota(jnp.int32, (CAP * groups, LANES), 0)
    sel_ref[...] = jnp.where(ri == column, 1.0, 0.0).astype(BF16)
    acc_ref[...] = jnp.zeros_like(acc_ref)

    def planes(ref, p):
        a, b = ref[2 * p], ref[2 * p + 1]
        return jnp.concatenate([a.reshape(PLANE, LANES), b.reshape(PLANE, LANES)], axis=1)

    def phase_a(p, carry):
        x = planes(x_ref, p).astype(BF16)
        y = mm(lhs1[...], jnp.concatenate([x, x], axis=0))
        for h in (0, 1):
            cols = slice(h * LANES, (h + 1) * LANES)
            z_ref[2 * p + h] = y[:PLANE, cols].reshape(SIDE, SIDE, LANES)
            kin_ref[2 * p + h] = y[PLANE:, cols].reshape(SIDE, SIDE, LANES)
        return carry

    for q in range(parts):
        copies_x[q].wait()
        lax.fori_loop(q * width // 2, (q + 1) * width // 2, phase_a, 0, unroll=True)
    for c in copies_p:
        c.wait()

    side = SIDE * HALF
    diag = diag_ref[...] * (1.0 / (LANES * groups))
    diag2 = jnp.concatenate([diag, diag], axis=1)
    ones = jnp.ones((2 * LANES, LANES), BF16)
    lane = lax.broadcasted_iota(jnp.int32, (HALF, LANES), 1)
    sub = lax.broadcasted_iota(jnp.int32, (HALF, LANES), 0)

    def column_pair(ref, j):
        s = ref[:, j]
        return jnp.concatenate(
            [s[:, :HALF].reshape(side, LANES), s[:, HALF:].reshape(side, LANES)], axis=1
        )

    def along_i(lhs, x):
        hi, lo = split2(x)
        y = mm(lhs[...], jnp.concatenate([hi, lo], axis=0))
        return y[:side] + y[side:]

    def uncolumn(y):
        return jnp.concatenate(
            [y[:, :LANES].reshape(SIDE, HALF, LANES), y[:, LANES:].reshape(SIDE, HALF, LANES)], axis=1
        )

    def phase_b(j, carry):
        r = along_i(lhs_f, column_pair(z_ref, j))
        x = column_pair(x_ref, j).astype(BF16)
        k = mm(lhs_k[...], jnp.concatenate([x, x], axis=0))
        v = along_i(lhs_ft, r * column_pair(pot_ref, j))
        v_ref[:, j] = uncolumn(v)
        kin_ref[:, j] += uncolumn(k)
        hi, lo = split2(diag2 * r * r)
        d = mm(
            jnp.concatenate(
                [
                    jnp.concatenate([hi[:, :LANES], lo[:, :LANES]], axis=1),
                    jnp.concatenate([hi[:, LANES:], lo[:, LANES:]], axis=1),
                ],
                axis=0,
            ),
            ones,
        )
        d = d.reshape(2, SIDE, HALF, LANES)
        base = jnp.bitwise_and(j, HALF - 1) * SIDE
        total = acc_ref[jnp.right_shift(j, 3)]
        for h in (0, 1):
            here = lane == sub + (base + h * HALF)
            total = total + jnp.where(here[None], d[h], 0.0)
        acc_ref[jnp.right_shift(j, 3)] = total
        return carry

    lax.fori_loop(0, SIDE, phase_b, 0, unroll=2)

    def gradient(p):
        g = mm(lhs_b[...], stack3(planes(v_ref, p))) + planes(kin_ref, p)
        grad_ref[p] = g.astype(BF16)

    def dispatch(p):
        for h in (0, 1):
            sent = lax.dot_general(
                sel_ref[...], grad_ref[p, :, h * LANES : (h + 1) * LANES], NT, preferred_element_type=F32
            )
            for c in (0, 1):
                rows_ref[:, 4 * p + 2 * h + c] = sent[:, c * LANES : (c + 1) * LANES].reshape(
                    CAP * groups // 8, 8, LANES
                )

    gradient(0)
    for p in range(1, SIDE // 2):
        gradient(p)
        dispatch(p - 1)
    dispatch(SIDE // 2 - 1)
    dens_ref[...] = jnp.concatenate([jnp.sum(acc_ref[0], axis=1), jnp.sum(acc_ref[1], axis=1)], axis=1)

    flat = rows_ref.reshape(CAP * groups * CHUNKS, LANES)
    bands = 4
    per = groups // bands

    def pack(g, carry):
        tile, within = jnp.right_shift(g, 3), jnp.bitwise_and(g, 7)
        for s in range(CAP):
            row = (s * (groups // 8) + tile) * (8 * CHUNKS) + within
            stage_ref[g, s * CHUNKS : (s + 1) * CHUNKS, :] = flat[pl.ds(row, CHUNKS, stride=8), :].astype(BF16)
        return carry

    outs = []
    for b in range(bands):
        lax.fori_loop(b * per, (b + 1) * per, pack, 0, unroll=8)
        part = pl.ds(b * per, per)
        outs.append(pltpu.make_async_copy(stage_ref.at[part], out_hbm.at[part], sem_o.at[b]))
        outs[-1].start()
    for c in outs:
        c.wait()


def run_apply(support, potential, magic_taps, kinetic_taps, kernel_diag, owners, groups):
    box = pltpu.VMEM((SIDE, SIDE, SIDE, LANES), F32)
    side = SIDE * HALF
    side_lhs = pltpu.VMEM((2 * side, 2 * side), BF16)
    dma = pltpu.SemaphoreType.DMA((4,))
    return pl.pallas_call(
        functools.partial(apply_kernel, groups),
        out_shape=(
            jax.ShapeDtypeStruct((groups, BLOCK, LANES), BF16),
            jax.ShapeDtypeStruct((SIDE, PLANE), F32),
        ),
        in_specs=[HBM] * 6,
        out_specs=(HBM, VM),
        scratch_shapes=[
            box, box, box, box, box,
            pltpu.VMEM((3, SIDE, PLANE), F32),
            pltpu.VMEM((2 * PLANE, 2 * PLANE), BF16),
            pltpu.VMEM((PLANE, 3 * PLANE), BF16),
            side_lhs, side_lhs,
            pltpu.VMEM((side, 2 * side), BF16),
            pltpu.VMEM((CAP * groups, LANES), BF16),
            pltpu.VMEM((CAP * groups // 8, CHUNKS, 8, LANES), F32),
            pltpu.VMEM((2, SIDE, HALF, LANES), F32),
            pltpu.VMEM((groups, BLOCK, LANES), BF16),
            pltpu.VMEM((SIDE // 2, PLANE, 2 * LANES), BF16),
            pltpu.SMEM((SIDE,), F32), pltpu.SMEM((SIDE,), F32),
            pltpu.VMEM((1, LANES), F32), pltpu.VMEM((1, LANES), jnp.int32),
            dma, dma, dma, dma,
        ],
        compiler_params=pltpu.CompilerParams(vmem_limit_bytes=67043328),
        name="apply",
    )(magic_taps, kinetic_taps, kernel_diag.reshape(1, LANES), owners.reshape(1, LANES), support, potential)


def select_kernel(groups, owner_ref, out_ref):
    owner = owner_ref[...]
    column = slot_of(owner) * groups + owner
    down = jnp.broadcast_to(column.astype(F32), (LANES, LANES)).T
    lane = lax.broadcasted_iota(jnp.int32, (LANES, LANES), 1).astype(F32)
    for t in range(CAP * groups // LANES + 1):
        out_ref[:, t * LANES : (t + 1) * LANES] = jnp.where(down == lane + float(t * LANES), 1.0, 0.0).astype(BF16)


def run_select(owners, groups):
    return pl.pallas_call(
        functools.partial(select_kernel, groups),
        out_shape=jax.ShapeDtypeStruct((LANES, 2 * LANES), BF16),
        in_specs=[VM],
        out_specs=VM,
        name="select",
    )(owners.reshape(1, LANES))


def margin_kernel(groups, recv_hbm, coef_ref, scale_ref, slab_ref, out_ref, recv_ref, rows_ref, sem):
    bands = 4
    per = groups // bands
    copies = []
    for b in range(bands):
        part = pl.ds(b * per, per)
        copies.append(pltpu.make_async_copy(recv_hbm.at[part], recv_ref.at[part], sem.at[b]))
        copies[-1].start()
    flat = rows_ref.reshape(CAP * groups * CHUNKS, LANES)

    def unpack(g, carry):
        tile, within = jnp.right_shift(g, 3), jnp.bitwise_and(g, 7)
        for s in range(CAP):
            row = (s * (groups // 8) + tile) * (8 * CHUNKS) + within
            flat[pl.ds(row, CHUNKS, stride=8), :] = recv_ref[g, s * CHUNKS : (s + 1) * CHUNKS, :].astype(F32)
        return carry

    for b in range(bands):
        copies[b].wait()
        lax.fori_loop(b * per, (b + 1) * per, unpack, 0, unroll=4)

    def step(i, acc):
        cols = [rows_ref[:, 2 * i + c].reshape(CAP * groups, LANES) for c in (0, 1)]
        lhs = jnp.concatenate(cols, axis=1).astype(BF16)
        return acc + mm(lhs, coef_ref[pl.ds(pl.multiple_of(i * PLANE, PLANE), PLANE), :])

    acc = lax.fori_loop(0, SIDE, step, jnp.zeros((CAP * groups, LANES), F32), unroll=4)
    acc = acc * (scale_ref[...] * (1.0 / float(SIDE) ** 1.5))
    for s in range(CAP):
        out_ref[pl.ds(s, groups, stride=BACK), :] = acc[s * groups : (s + 1) * groups]
    slab = slab_ref[...]
    for h in range(2):
        out_ref[pl.ds(CAP + h, groups, stride=BACK), :] = jnp.broadcast_to(
            slab[:, h * LANES : (h + 1) * LANES], (groups, LANES)
        )
    for s in range(CAP + 2, BACK):
        out_ref[pl.ds(s, groups, stride=BACK), :] = jnp.zeros((groups, LANES), F32)


def run_margin(received, owned, kernel_diag, slab, groups):
    return pl.pallas_call(
        functools.partial(margin_kernel, groups),
        out_shape=jax.ShapeDtypeStruct((groups * BACK, LANES), F32),
        in_specs=[HBM, VM, VM, VM],
        out_specs=VM,
        scratch_shapes=[
            pltpu.VMEM((groups, BLOCK, LANES), BF16),
            pltpu.VMEM((CAP * groups // 8, CHUNKS, 8, LANES), F32),
            pltpu.SemaphoreType.DMA((4,)),
        ],
        compiler_params=pltpu.CompilerParams(vmem_limit_bytes=16 * 1024 * 1024),
        name="margin",
    )(received, owned, kernel_diag.reshape(1, LANES), slab)


def gather_kernel(groups, select_ref, ret_ref, out_ref, dens_ref):
    rows = [ret_ref[pl.ds(s, groups, stride=BACK), :] for s in range(CAP + 2)]
    x = jnp.concatenate(rows[:CAP] + [jnp.zeros((groups, LANES), F32)], axis=0)
    hi, mid = split2(x)
    lo = (x - hi.astype(F32) - mid.astype(F32)).astype(BF16)
    y = mm(select_ref[...], jnp.concatenate([hi, mid], axis=1))
    out_ref[...] = y[:, :LANES] + (y[:, LANES:] + mm(select_ref[...], lo))
    for h in range(2):
        dens_ref[:, h * LANES : (h + 1) * LANES] = jnp.sum(
            rows[CAP + h].reshape(groups // HALF, HALF, LANES), axis=0
        )


def run_gather(select, returned, groups):
    return pl.pallas_call(
        functools.partial(gather_kernel, groups),
        out_shape=(
            jax.ShapeDtypeStruct((LANES, LANES), F32),
            jax.ShapeDtypeStruct((HALF, PLANE), F32),
        ),
        in_specs=[VM, VM],
        out_specs=(VM, VM),
        name="gather",
    )(select, returned)


def body(support, potential, magic_taps, kinetic_taps, kernel_diag, owners):
    groups = lax.axis_size("grp")
    domains = lax.axis_size("dom")
    outgoing, part = run_apply(support, potential, magic_taps, kinetic_taps, kernel_diag, owners, groups)
    received = lax.all_to_all(outgoing, "grp", split_axis=0, concat_axis=0, tiled=True)
    owners_late, support_late, part = lax.optimization_barrier((owners, support, part))
    select = run_select(owners_late, groups)
    owned = support_late.reshape(CELLS, LANES).astype(BF16)
    distance = 1
    while distance < HALF:
        part = part + lax.ppermute(part, "grp", [(i, i ^ distance) for i in range(groups)])
        distance *= 2
    upper = lax.ppermute(part[HALF:], "dom", [(i, (i + 1) % domains) for i in range(domains)])
    mine = lax.axis_index("grp") % HALF
    slab = lax.dynamic_slice_in_dim(part[:HALF] + upper, mine, 1, 0)
    products = run_margin(received, owned, kernel_diag, slab, groups)
    returned = lax.all_to_all(
        products.reshape(groups, BACK, LANES), "grp", split_axis=0, concat_axis=0, tiled=True
    )
    return run_gather(select, returned.reshape(groups * BACK, LANES), groups)


def solution(mesh):
    return jax.shard_map(
        body,
        mesh=mesh,
        in_specs=(
            P(None, None, None, ("dom", "grp")),
            P(None, None, None, ("dom", "grp")),
            P(),
            P(),
            P(("dom", "grp")),
            P(("dom", "grp"), None),
        ),
        out_specs=(P(("dom", "grp"), None), P("dom", None)),
        check_vma=False,
    )
```

```python
import functools

import jax
import jax.numpy as jnp
from jax import lax
from jax.experimental import pallas as pl
from jax.experimental.pallas import tpu as pltpu
from jax.sharding import PartitionSpec as P

F32 = jnp.float32
BF16 = jnp.bfloat16
SIDE = 16
HALF = SIDE // 2
PLANE = SIDE * SIDE
CELLS = SIDE**3
LANES = 128
CAP = 3
CHUNKS = CELLS // LANES
BLOCK = CAP * CHUNKS
BACK = 8
NT = (((1,), (1,)), ((), ()))

VM = pl.BlockSpec(memory_space=pltpu.VMEM)
HBM = pl.BlockSpec(memory_space=pltpu.HBM)


def split2(x):
    hi = x.astype(BF16)
    lo = (x - hi.astype(F32)).astype(BF16)
    return hi, lo


def mm(a, b):
    return jnp.dot(a, b, preferred_element_type=F32)


def tap_lookup(taps_ref, offset):
    out = jnp.zeros(offset.shape, F32)
    for q in range(SIDE):
        out = jnp.where(offset == q, taps_ref[q], out)
    return out


def stack3(x):
    hi, lo = split2(x)
    return jnp.concatenate([hi, hi, lo], axis=0)


def slot_of(owner_row):
    n = owner_row.shape[1]
    across = jnp.broadcast_to(owner_row.astype(F32), (n, n))
    down = across.T
    r = lax.broadcasted_iota(jnp.int32, (n, n), 0)
    c = lax.broadcasted_iota(jnp.int32, (n, n), 1)
    earlier = jnp.where((across == down) & (r < c), 1.0, 0.0)
    return jnp.sum(earlier, axis=0, keepdims=True).astype(jnp.int32)


def build_plane_matrices(magic, kinetic, pat_ref, lhs1, lhs_b):
    half = SIDE // 2 - 1
    a = lax.broadcasted_iota(jnp.int32, (SIDE, PLANE), 0)
    c = lax.broadcasted_iota(jnp.int32, (SIDE, PLANE), 1)
    minor = jnp.bitwise_and(c, SIDE - 1) - a
    major = jnp.right_shift(c, 4) - a
    f_minor = tap_lookup(magic, minor + half)
    k_minor = tap_lookup(kinetic, minor + half)
    ft_minor = tap_lookup(magic, half - minor)
    pat_ref[0] = tap_lookup(magic, major + half)
    pat_ref[1] = tap_lookup(kinetic, major + half)
    pat_ref[2] = tap_lookup(magic, half - major)
    same_minor = minor == 0
    lane_major = jnp.right_shift(c, 4)

    def put(dst, row, mat, third):
        hi, lo = split2(mat)
        dst[pl.ds(row, SIDE), 0:PLANE] = hi
        dst[pl.ds(row, SIDE), PLANE : 2 * PLANE] = lo
        if third:
            dst[pl.ds(row, SIDE), 2 * PLANE : 3 * PLANE] = hi

    def rows(g, carry):
        r = pl.multiple_of(g * SIDE, SIDE)
        fm = pat_ref[0, pl.ds(g, 1), :]
        km = pat_ref[1, pl.ds(g, 1), :]
        bm = pat_ref[2, pl.ds(g, 1), :]
        put(lhs1, r, fm * f_minor, False)
        put(lhs1, r + PLANE, jnp.where(same_minor, km, 0.0) + jnp.where(lane_major == g, k_minor, 0.0), False)
        put(lhs_b, r, bm * ft_minor, True)
        return carry

    lax.fori_loop(0, SIDE, rows, 0)


def build_side_matrix(taps, lhs, transposed, double):
    n = SIDE * HALF
    half = SIDE // 2 - 1
    r = lax.broadcasted_iota(jnp.int32, (n, n), 0)
    c = lax.broadcasted_iota(jnp.int32, (n, n), 1)
    delta = jnp.right_shift(c, 3) - jnp.right_shift(r, 3)
    offset = half - delta if transposed else delta + half
    same = jnp.bitwise_and(r, HALF - 1) == jnp.bitwise_and(c, HALF - 1)
    hi, lo = split2(tap_lookup(taps, jnp.where(same, offset, -1)))
    lhs[0:n, 0:n] = hi
    if not double:
        lhs[0:n, n : 2 * n] = lo
        return
    lhs[0:n, n : 2 * n] = hi
    lhs[n : 2 * n, 0:n] = lo
    lhs[n : 2 * n, n : 2 * n] = lo


def apply_kernel(
    groups,
    magic_hbm, kinetic_hbm, diag_hbm, owner_hbm, x_hbm, pot_hbm,
    out_hbm, dens_ref,
    x_ref, pot_ref, z_ref, kin_ref, kin_i_ref, r_ref, v_ref,
    pat_ref, lhs1, lhs_b, lhs_f, lhs_ft, lhs_k, sel_ref, rows_ref, stage_ref, grad_ref,
    magic, kinetic, diag_ref, owner_ref,
    sem_s, sem_x, sem_p, sem_o,
):
    small = [
        pltpu.make_async_copy(src, dst, sem_s.at[q])
        for q, (src, dst) in enumerate(
            [(magic_hbm, magic), (kinetic_hbm, kinetic), (diag_hbm, diag_ref), (owner_hbm, owner_ref)]
        )
    ]
    parts = 4
    width = SIDE // parts
    copies_x, copies_p = [], []
    for q in range(parts):
        part = pl.ds(q * width, width)
        copies_x.append(pltpu.make_async_copy(x_hbm.at[part], x_ref.at[part], sem_x.at[q]))
        copies_p.append(pltpu.make_async_copy(pot_hbm.at[part], pot_ref.at[part], sem_p.at[q]))
    for c in small + copies_x + copies_p:
        c.start()
    for c in small:
        c.wait()

    build_plane_matrices(magic, kinetic, pat_ref, lhs1, lhs_b)
    build_side_matrix(magic, lhs_f, False, True)
    build_side_matrix(magic, lhs_ft, True, True)
    build_side_matrix(kinetic, lhs_k, False, False)
    owner = owner_ref[...]
    column = slot_of(owner) * groups + owner
    ri = lax.broadcasted_iota(jnp.int32, (CAP * groups, LANES), 0)
    sel_ref[...] = jnp.where(ri == column, 1.0, 0.0).astype(BF16)

    def planes(ref, p):
        a, b = ref[2 * p], ref[2 * p + 1]
        return jnp.concatenate([a.reshape(PLANE, LANES), b.reshape(PLANE, LANES)], axis=1)

    def phase_a(p, carry):
        x = planes(x_ref, p).astype(BF16)
        y = mm(lhs1[...], jnp.concatenate([x, x], axis=0))
        for h in (0, 1):
            cols = slice(h * LANES, (h + 1) * LANES)
            z_ref[2 * p + h] = y[:PLANE, cols].reshape(SIDE, SIDE, LANES)
            kin_ref[2 * p + h] = y[PLANE:, cols].reshape(SIDE, SIDE, LANES)
        return carry

    for c in copies_x:
        c.wait()
    lax.fori_loop(0, SIDE // 2, phase_a, 0, unroll=4)
    for c in copies_p:
        c.wait()

    side = SIDE * HALF
    diag = diag_ref[...] * (1.0 / (LANES * groups))
    diag2 = jnp.concatenate([diag, diag], axis=1)
    lane = lax.broadcasted_iota(jnp.int32, (HALF, LANES), 1)
    sub = lax.broadcasted_iota(jnp.int32, (HALF, LANES), 0)

    def column_pair(ref, j):
        s = ref[:, j]
        return jnp.concatenate(
            [s[:, :HALF].reshape(side, LANES), s[:, HALF:].reshape(side, LANES)], axis=1
        )

    def along_i(lhs, x):
        hi, lo = split2(x)
        y = mm(lhs[...], jnp.concatenate([hi, lo], axis=0))
        return y[:side] + y[side:]

    def filter_out(j):
        r_ref[j] = along_i(lhs_f, column_pair(z_ref, j))
        x = column_pair(x_ref, j).astype(BF16)
        kin_i_ref[j] = mm(lhs_k[...], jnp.concatenate([x, x], axis=0))

    def filter_back(j, total):
        r = r_ref[j]
        v_ref[j] = along_i(lhs_ft, r * column_pair(pot_ref, j))
        weighted = diag2 * r * r
        for h in (0, 1):
            here = lane == sub + (jnp.bitwise_and(j, HALF - 1) * SIDE + h * HALF)
            d = jnp.sum(weighted[:, h * LANES : (h + 1) * LANES], axis=1, keepdims=True)
            d = jnp.broadcast_to(d, (side, LANES)).reshape(SIDE, HALF, LANES)
            total = total + jnp.where(here[None], d, 0.0)
        return total

    filter_out(0)
    total = jnp.zeros((SIDE, HALF, LANES), F32)
    for j in range(SIDE):
        if j + 1 < SIDE:
            filter_out(j + 1)
        total = filter_back(j, total)
        if j % HALF == HALF - 1:
            t = j // HALF
            dens_ref[:, t * LANES : (t + 1) * LANES] = jnp.sum(total, axis=1)
            total = jnp.zeros((SIDE, HALF, LANES), F32)

    def slab_planes(ref, p):
        def one(i):
            rows = pl.ds(i * HALF, HALF)
            both = [ref[:, rows, h * LANES : (h + 1) * LANES] for h in (0, 1)]
            return jnp.concatenate(both, axis=1).reshape(PLANE, LANES)

        return jnp.concatenate([one(2 * p), one(2 * p + 1)], axis=1)

    def gradient(p):
        g = mm(lhs_b[...], stack3(slab_planes(v_ref, p))) + (planes(kin_ref, p) + slab_planes(kin_i_ref, p))
        grad_ref[p] = g.astype(BF16)

    def dispatch(p):
        for h in (0, 1):
            sent = lax.dot_general(
                sel_ref[...], grad_ref[p, :, h * LANES : (h + 1) * LANES], NT, preferred_element_type=F32
            )
            for c in (0, 1):
                chunk = 4 * p + 2 * h + c
                place = chunk // 8 * 64 + chunk % 8
                for t in range(CAP * groups // 8):
                    rows_ref[pl.ds(place + t * 8 * CHUNKS, 8, stride=8), :] = sent[
                        t * 8 : t * 8 + 8, c * LANES : (c + 1) * LANES
                    ]

    def stage(p, carry):
        gradient(p)
        dispatch(p - 1)
        return carry

    gradient(0)
    for p in range(1, SIDE // 2):
        stage(p, 0)
    dispatch(SIDE // 2 - 1)
    bands = 4
    per = groups // bands

    def pack(g):
        tile, within = g // 8, g % 8
        for s in range(CAP):
            row = (s * (groups // 8) + tile) * (8 * CHUNKS) + within * 8
            parts = [rows_ref[pl.ds(row + q * 64, 8), :] for q in range(CHUNKS // 8)]
            stage_ref[g, s * CHUNKS : (s + 1) * CHUNKS, :] = jnp.concatenate(parts, axis=0).astype(BF16)

    outs = []
    for b in range(bands):
        for g in range(b * per, (b + 1) * per):
            pack(g)
        part = pl.ds(b * per, per)
        outs.append(pltpu.make_async_copy(stage_ref.at[part], out_hbm.at[part], sem_o.at[b]))
        outs[-1].start()
    for c in outs:
        c.wait()


def run_apply(support, potential, magic_taps, kinetic_taps, kernel_diag, owners, groups):
    box = pltpu.VMEM((SIDE, SIDE, SIDE, LANES), F32)
    side = SIDE * HALF
    slab = pltpu.VMEM((SIDE, side, 2 * LANES), F32)
    side_lhs = pltpu.VMEM((2 * side, 2 * side), BF16)
    dma = pltpu.SemaphoreType.DMA((4,))
    return pl.pallas_call(
        functools.partial(apply_kernel, groups),
        out_shape=(
            jax.ShapeDtypeStruct((groups, BLOCK, LANES), BF16),
            jax.ShapeDtypeStruct((SIDE, PLANE), F32),
        ),
        in_specs=[HBM] * 6,
        out_specs=(HBM, VM),
        scratch_shapes=[
            box, box, box, box, slab, slab, slab,
            pltpu.VMEM((3, SIDE, PLANE), F32),
            pltpu.VMEM((2 * PLANE, 2 * PLANE), BF16),
            pltpu.VMEM((PLANE, 3 * PLANE), BF16),
            side_lhs, side_lhs,
            pltpu.VMEM((side, 2 * side), BF16),
            pltpu.VMEM((CAP * groups, LANES), BF16),
            pltpu.VMEM((CAP * groups * CHUNKS, LANES), F32),
            pltpu.VMEM((groups, BLOCK, LANES), BF16),
            pltpu.VMEM((SIDE // 2, PLANE, 2 * LANES), BF16),
            pltpu.SMEM((SIDE,), F32), pltpu.SMEM((SIDE,), F32),
            pltpu.VMEM((1, LANES), F32), pltpu.VMEM((1, LANES), jnp.int32),
            dma, dma, dma, dma,
        ],
        compiler_params=pltpu.CompilerParams(vmem_limit_bytes=67043328),
        name="apply",
    )(magic_taps, kinetic_taps, kernel_diag.reshape(1, LANES), owners.reshape(1, LANES), support, potential)


def select_kernel(groups, owner_ref, out_ref):
    owner = owner_ref[...]
    column = slot_of(owner) * groups + owner
    down = jnp.broadcast_to(column.astype(F32), (LANES, LANES)).T
    lane = lax.broadcasted_iota(jnp.int32, (LANES, LANES), 1).astype(F32)
    for t in range(CAP * groups // LANES + 1):
        out_ref[:, t * LANES : (t + 1) * LANES] = jnp.where(down == lane + float(t * LANES), 1.0, 0.0).astype(BF16)


def run_select(owners, groups):
    return pl.pallas_call(
        functools.partial(select_kernel, groups),
        out_shape=jax.ShapeDtypeStruct((LANES, 2 * LANES), BF16),
        in_specs=[VM],
        out_specs=VM,
        name="select",
    )(owners.reshape(1, LANES))


def margin_kernel(groups, recv_ref, coef_ref, scale_ref, slab_ref, out_ref, rows_ref):
    for g in range(groups):
        for s in range(CAP):
            block = recv_ref[g, s * CHUNKS : (s + 1) * CHUNKS, :].astype(F32)
            row = (s * (groups // 8) + g // 8) * (8 * CHUNKS) + g % 8 * 8
            for q in range(CHUNKS // 8):
                rows_ref[pl.ds(row + q * 64, 8), :] = block[q * 8 : q * 8 + 8]

    def column(c):
        start = c // 8 * 64 + c % 8
        tiles = [
            rows_ref[pl.ds(start + t * 8 * CHUNKS, 8, stride=8), :] for t in range(CAP * groups // 8)
        ]
        return jnp.concatenate(tiles, axis=0)

    acc = jnp.zeros((CAP * groups, LANES), F32)
    for i in range(SIDE):
        lhs = jnp.concatenate([column(2 * i), column(2 * i + 1)], axis=1).astype(BF16)
        acc = acc + mm(lhs, coef_ref[i * PLANE : (i + 1) * PLANE, :])
    acc = acc * (scale_ref[...] * (1.0 / float(SIDE) ** 1.5))
    for s in range(CAP):
        out_ref[pl.ds(s, groups, stride=BACK), :] = acc[s * groups : (s + 1) * groups]
    slab = slab_ref[...]
    for h in range(2):
        out_ref[pl.ds(CAP + h, groups, stride=BACK), :] = jnp.broadcast_to(
            slab[:, h * LANES : (h + 1) * LANES], (groups, LANES)
        )
    for s in range(CAP + 2, BACK):
        out_ref[pl.ds(s, groups, stride=BACK), :] = jnp.zeros((groups, LANES), F32)


def run_margin(received, owned, kernel_diag, slab, groups):
    return pl.pallas_call(
        functools.partial(margin_kernel, groups),
        out_shape=jax.ShapeDtypeStruct((groups * BACK, LANES), F32),
        in_specs=[VM, VM, VM, VM],
        out_specs=VM,
        scratch_shapes=[pltpu.VMEM((CAP * groups * CHUNKS, LANES), F32)],
        compiler_params=pltpu.CompilerParams(vmem_limit_bytes=16 * 1024 * 1024),
        name="margin",
    )(received, owned, kernel_diag.reshape(1, LANES), slab)


def gather_kernel(groups, select_ref, ret_hbm, out_ref, dens_ref, ret_ref, sem):
    copy = pltpu.make_async_copy(ret_hbm, ret_ref, sem)
    copy.start()
    copy.wait()
    rows = [ret_ref[pl.ds(s, groups, stride=BACK), :] for s in range(CAP + 2)]
    x = jnp.concatenate(rows[:CAP] + [jnp.zeros((groups, LANES), F32)], axis=0)
    hi, mid = split2(x)
    lo = (x - hi.astype(F32) - mid.astype(F32)).astype(BF16)
    y = mm(select_ref[...], jnp.concatenate([hi, mid], axis=1))
    out_ref[...] = y[:, :LANES] + (y[:, LANES:] + mm(select_ref[...], lo))
    for h in range(2):
        dens_ref[:, h * LANES : (h + 1) * LANES] = jnp.sum(
            rows[CAP + h].reshape(groups // HALF, HALF, LANES), axis=0
        )


def run_gather(select, returned, groups):
    return pl.pallas_call(
        functools.partial(gather_kernel, groups),
        out_shape=(
            jax.ShapeDtypeStruct((LANES, LANES), F32),
            jax.ShapeDtypeStruct((HALF, PLANE), F32),
        ),
        in_specs=[VM, HBM],
        out_specs=(VM, VM),
        scratch_shapes=[
            pltpu.VMEM((groups * BACK, LANES), F32),
            pltpu.SemaphoreType.DMA,
        ],
        compiler_params=pltpu.CompilerParams(vmem_limit_bytes=4 * 1024 * 1024),
        name="gather",
    )(select, returned)


def body(support, potential, magic_taps, kinetic_taps, kernel_diag, owners):
    groups = lax.axis_size("grp")
    domains = lax.axis_size("dom")
    outgoing, part = run_apply(support, potential, magic_taps, kinetic_taps, kernel_diag, owners, groups)
    received = lax.all_to_all(outgoing, "grp", split_axis=0, concat_axis=0, tiled=True)
    owners_late, support_late, part = lax.optimization_barrier((owners, support, part))
    select = run_select(owners_late, groups)
    owned = support_late.reshape(CELLS, LANES).astype(BF16)
    distance = 1
    while distance < HALF:
        part = part + lax.ppermute(part, "grp", [(i, i ^ distance) for i in range(groups)])
        distance *= 2
    upper = lax.ppermute(part[HALF:], "dom", [(i, (i + 1) % domains) for i in range(domains)])
    mine = lax.axis_index("grp") % HALF
    slab = lax.dynamic_slice_in_dim(part[:HALF] + upper, mine, 1, 0)
    products = run_margin(received, owned, kernel_diag, slab, groups)
    returned = lax.all_to_all(
        products.reshape(groups, BACK, LANES), "grp", split_axis=0, concat_axis=0, tiled=True
    )
    return run_gather(select, returned.reshape(groups * BACK, LANES), groups)


def solution(mesh):
    return jax.shard_map(
        body,
        mesh=mesh,
        in_specs=(
            P(None, None, None, ("dom", "grp")),
            P(None, None, None, ("dom", "grp")),
            P(),
            P(),
            P(("dom", "grp")),
            P(("dom", "grp"), None),
        ),
        out_specs=(P(("dom", "grp"), None), P("dom", None)),
        check_vma=False,
    )
```

```python
import functools

import jax
import jax.numpy as jnp
from jax import lax
from jax.experimental import pallas as pl
from jax.experimental.pallas import tpu as pltpu
from jax.sharding import PartitionSpec as P

F32 = jnp.float32
BF16 = jnp.bfloat16
SIDE = 16
HALF = SIDE // 2
PLANE = SIDE * SIDE
CELLS = SIDE**3
LANES = 128
CAP = 3
CHUNKS = CELLS // LANES
BLOCK = CAP * CHUNKS
BACK = CAP + 2
NT = (((1,), (1,)), ((), ()))

VM = pl.BlockSpec(memory_space=pltpu.VMEM)
HBM = pl.BlockSpec(memory_space=pltpu.HBM)


def split2(x):
    hi = x.astype(BF16)
    lo = (x - hi.astype(F32)).astype(BF16)
    return hi, lo


def mm(a, b):
    return jnp.dot(a, b, preferred_element_type=F32)


def tap_lookup(taps_ref, offset):
    out = jnp.zeros(offset.shape, F32)
    for q in range(SIDE):
        out = jnp.where(offset == q, taps_ref[q], out)
    return out


def stack3(x):
    hi, lo = split2(x)
    return jnp.concatenate([hi, hi, lo], axis=0)


def slot_of(owner_row):
    n = owner_row.shape[1]
    across = jnp.broadcast_to(owner_row.astype(F32), (n, n))
    down = across.T
    r = lax.broadcasted_iota(jnp.int32, (n, n), 0)
    c = lax.broadcasted_iota(jnp.int32, (n, n), 1)
    earlier = jnp.where((across == down) & (r < c), 1.0, 0.0)
    return jnp.sum(earlier, axis=0, keepdims=True).astype(jnp.int32)


def build_plane_matrices(magic, kinetic, pat_ref, lhs1, lhs_b):
    half = SIDE // 2 - 1
    a = lax.broadcasted_iota(jnp.int32, (SIDE, PLANE), 0)
    c = lax.broadcasted_iota(jnp.int32, (SIDE, PLANE), 1)
    minor = jnp.bitwise_and(c, SIDE - 1) - a
    major = jnp.right_shift(c, 4) - a
    f_minor = tap_lookup(magic, minor + half)
    k_minor = tap_lookup(kinetic, minor + half)
    ft_minor = tap_lookup(magic, half - minor)
    pat_ref[0] = tap_lookup(magic, major + half)
    pat_ref[1] = tap_lookup(kinetic, major + half)
    pat_ref[2] = tap_lookup(magic, half - major)
    same_minor = minor == 0
    lane_major = jnp.right_shift(c, 4)

    def put(dst, row, mat, third):
        hi, lo = split2(mat)
        dst[pl.ds(row, SIDE), 0:PLANE] = hi
        dst[pl.ds(row, SIDE), PLANE : 2 * PLANE] = lo
        if third:
            dst[pl.ds(row, SIDE), 2 * PLANE : 3 * PLANE] = hi

    def rows(g, carry):
        r = pl.multiple_of(g * SIDE, SIDE)
        fm = pat_ref[0, pl.ds(g, 1), :]
        km = pat_ref[1, pl.ds(g, 1), :]
        bm = pat_ref[2, pl.ds(g, 1), :]
        put(lhs1, r, fm * f_minor, False)
        put(lhs1, r + PLANE, jnp.where(same_minor, km, 0.0) + jnp.where(lane_major == g, k_minor, 0.0), False)
        put(lhs_b, r, bm * ft_minor, True)
        return carry

    lax.fori_loop(0, SIDE, rows, 0)


def build_side_matrix(taps, lhs, transposed, double):
    n = SIDE * HALF
    half = SIDE // 2 - 1
    a = lax.broadcasted_iota(jnp.int32, (SIDE, n), 0)
    c = lax.broadcasted_iota(jnp.int32, (SIDE, n), 1)
    delta = jnp.right_shift(c, 3) - a
    pattern = tap_lookup(taps, half - delta if transposed else delta + half)
    sub = lax.broadcasted_iota(jnp.int32, (HALF, n), 0)
    lane = lax.broadcasted_iota(jnp.int32, (HALF, n), 1)
    same = sub == jnp.bitwise_and(lane, HALF - 1)
    full = jnp.concatenate([jnp.where(same, pattern[i : i + 1], 0.0) for i in range(SIDE)], axis=0)
    hi, lo = split2(full)
    lhs[0:n, 0:n] = hi
    if not double:
        lhs[0:n, n : 2 * n] = lo
        return
    lhs[0:n, n : 2 * n] = hi
    lhs[n : 2 * n, 0:n] = lo
    lhs[n : 2 * n, n : 2 * n] = lo


def apply_kernel(
    groups,
    magic_hbm, kinetic_hbm, diag_hbm, owner_hbm, x_hbm, pot_hbm,
    out_hbm, dens_ref,
    x_ref, pot_ref, z_ref, kin_ref, kin_i_ref, r_ref, v_ref,
    pat_ref, lhs1, lhs_b, lhs_f, lhs_ft, lhs_k, sel_ref, rows_ref, stage_ref, grad_ref,
    magic, kinetic, diag_ref, owner_ref,
    sem_s, sem_x, sem_p, sem_o,
):
    small = [
        pltpu.make_async_copy(src, dst, sem_s.at[q])
        for q, (src, dst) in enumerate(
            [(magic_hbm, magic), (kinetic_hbm, kinetic), (diag_hbm, diag_ref), (owner_hbm, owner_ref)]
        )
    ]
    parts = 4
    width = SIDE // parts
    copies_x, copies_p = [], []
    for q in range(parts):
        part = pl.ds(q * width, width)
        copies_x.append(pltpu.make_async_copy(x_hbm.at[part], x_ref.at[part], sem_x.at[q]))
        copies_p.append(pltpu.make_async_copy(pot_hbm.at[part], pot_ref.at[part], sem_p.at[q]))
    for c in small + copies_x + copies_p:
        c.start()
    for c in small:
        c.wait()

    build_plane_matrices(magic, kinetic, pat_ref, lhs1, lhs_b)
    build_side_matrix(magic, lhs_f, False, True)
    build_side_matrix(magic, lhs_ft, True, True)
    build_side_matrix(kinetic, lhs_k, False, False)
    owner = owner_ref[...]
    column = slot_of(owner) * groups + owner
    ri = lax.broadcasted_iota(jnp.int32, (CAP * groups, LANES), 0)
    sel_ref[...] = jnp.where(ri == column, 1.0, 0.0).astype(BF16)

    def planes(ref, p):
        a, b = ref[2 * p], ref[2 * p + 1]
        return jnp.concatenate([a.reshape(PLANE, LANES), b.reshape(PLANE, LANES)], axis=1)

    def phase_a(p, carry):
        x = planes(x_ref, p).astype(BF16)
        y = mm(lhs1[...], jnp.concatenate([x, x], axis=0))
        for h in (0, 1):
            cols = slice(h * LANES, (h + 1) * LANES)
            z_ref[2 * p + h] = y[:PLANE, cols].reshape(SIDE, SIDE, LANES)
            kin_ref[2 * p + h] = y[PLANE:, cols].reshape(SIDE, SIDE, LANES)
        return carry

    for c in copies_x:
        c.wait()
    lax.fori_loop(0, SIDE // 2, phase_a, 0, unroll=4)
    for c in copies_p:
        c.wait()

    side = SIDE * HALF
    diag = diag_ref[...] * (1.0 / (LANES * groups))
    diag2 = jnp.concatenate([diag, diag], axis=1)
    lane = lax.broadcasted_iota(jnp.int32, (HALF, LANES), 1)
    sub = lax.broadcasted_iota(jnp.int32, (HALF, LANES), 0)

    def column_pair(ref, j):
        s = ref[:, j]
        return jnp.concatenate(
            [s[:, :HALF].reshape(side, LANES), s[:, HALF:].reshape(side, LANES)], axis=1
        )

    def along_i(lhs, x):
        hi, lo = split2(x)
        y = mm(lhs[...], jnp.concatenate([hi, lo], axis=0))
        return y[:side] + y[side:]

    def filter_out(j):
        r_ref[j] = along_i(lhs_f, column_pair(z_ref, j))
        x = column_pair(x_ref, j).astype(BF16)
        kin_i_ref[j] = mm(lhs_k[...], jnp.concatenate([x, x], axis=0))

    def filter_back(j, total):
        r = r_ref[j]
        v_ref[j] = along_i(lhs_ft, r * column_pair(pot_ref, j))
        weighted = diag2 * r * r
        for h in (0, 1):
            here = lane == sub + (jnp.bitwise_and(j, HALF - 1) * SIDE + h * HALF)
            d = jnp.sum(weighted[:, h * LANES : (h + 1) * LANES], axis=1, keepdims=True)
            d = jnp.broadcast_to(d, (side, LANES)).reshape(SIDE, HALF, LANES)
            total = total + jnp.where(here[None], d, 0.0)
        return total

    filter_out(0)
    total = jnp.zeros((SIDE, HALF, LANES), F32)
    for j in range(SIDE):
        if j + 1 < SIDE:
            filter_out(j + 1)
        total = filter_back(j, total)
        if j % HALF == HALF - 1:
            t = j // HALF
            dens_ref[:, t * LANES : (t + 1) * LANES] = jnp.sum(total, axis=1)
            total = jnp.zeros((SIDE, HALF, LANES), F32)

    def slab_planes(ref, p):
        def one(i):
            rows = pl.ds(i * HALF, HALF)
            both = [ref[:, rows, h * LANES : (h + 1) * LANES] for h in (0, 1)]
            return jnp.concatenate(both, axis=1).reshape(PLANE, LANES)

        return jnp.concatenate([one(2 * p), one(2 * p + 1)], axis=1)

    def gradient(p):
        g = mm(lhs_b[...], stack3(slab_planes(v_ref, p))) + (planes(kin_ref, p) + slab_planes(kin_i_ref, p))
        grad_ref[p] = g.astype(BF16)

    def dispatch(p):
        for h in (0, 1):
            sent = lax.dot_general(
                sel_ref[...], grad_ref[p, :, h * LANES : (h + 1) * LANES], NT, preferred_element_type=F32
            )
            for c in (0, 1):
                chunk = 4 * p + 2 * h + c
                place = chunk // 8 * 64 + chunk % 8
                for t in range(CAP * groups // 8):
                    rows_ref[pl.ds(place + t * 8 * CHUNKS, 8, stride=8), :] = sent[
                        t * 8 : t * 8 + 8, c * LANES : (c + 1) * LANES
                    ]

    def stage(p, carry):
        gradient(p)
        dispatch(p - 1)
        return carry

    gradient(0)
    for p in range(1, SIDE // 2):
        stage(p, 0)
    dispatch(SIDE // 2 - 1)
    bands = 4
    per = groups // bands

    def pack(g):
        tile, within = g // 8, g % 8
        for s in range(CAP):
            row = (s * (groups // 8) + tile) * (8 * CHUNKS) + within * 8
            parts = [rows_ref[pl.ds(row + q * 64, 8), :] for q in range(CHUNKS // 8)]
            stage_ref[g, s * CHUNKS : (s + 1) * CHUNKS, :] = jnp.concatenate(parts, axis=0).astype(BF16)

    outs = []
    for b in range(bands):
        for g in range(b * per, (b + 1) * per):
            pack(g)
        part = pl.ds(b * per, per)
        outs.append(pltpu.make_async_copy(stage_ref.at[part], out_hbm.at[part], sem_o.at[b]))
        outs[-1].start()
    for c in outs:
        c.wait()


def run_apply(support, potential, magic_taps, kinetic_taps, kernel_diag, owners, groups):
    box = pltpu.VMEM((SIDE, SIDE, SIDE, LANES), F32)
    side = SIDE * HALF
    slab = pltpu.VMEM((SIDE, side, 2 * LANES), F32)
    side_lhs = pltpu.VMEM((2 * side, 2 * side), BF16)
    dma = pltpu.SemaphoreType.DMA((4,))
    return pl.pallas_call(
        functools.partial(apply_kernel, groups),
        out_shape=(
            jax.ShapeDtypeStruct((groups, BLOCK, LANES), BF16),
            jax.ShapeDtypeStruct((SIDE, PLANE), F32),
        ),
        in_specs=[HBM] * 6,
        out_specs=(HBM, VM),
        scratch_shapes=[
            box, box, box, box, slab, slab, slab,
            pltpu.VMEM((3, SIDE, PLANE), F32),
            pltpu.VMEM((2 * PLANE, 2 * PLANE), BF16),
            pltpu.VMEM((PLANE, 3 * PLANE), BF16),
            side_lhs, side_lhs,
            pltpu.VMEM((side, 2 * side), BF16),
            pltpu.VMEM((CAP * groups, LANES), BF16),
            pltpu.VMEM((CAP * groups * CHUNKS, LANES), F32),
            pltpu.VMEM((groups, BLOCK, LANES), BF16),
            pltpu.VMEM((SIDE // 2, PLANE, 2 * LANES), BF16),
            pltpu.SMEM((SIDE,), F32), pltpu.SMEM((SIDE,), F32),
            pltpu.VMEM((1, LANES), F32), pltpu.VMEM((1, LANES), jnp.int32),
            dma, dma, dma, dma,
        ],
        compiler_params=pltpu.CompilerParams(vmem_limit_bytes=67043328),
        name="apply",
    )(magic_taps, kinetic_taps, kernel_diag.reshape(1, LANES), owners.reshape(1, LANES), support, potential)


def select_kernel(groups, owner_ref, out_ref):
    owner = owner_ref[...]
    column = slot_of(owner) * groups + owner
    down = jnp.broadcast_to(column.astype(F32), (LANES, LANES)).T
    lane = lax.broadcasted_iota(jnp.int32, (LANES, LANES), 1).astype(F32)
    for t in range(CAP * groups // LANES + 1):
        out_ref[:, t * LANES : (t + 1) * LANES] = jnp.where(down == lane + float(t * LANES), 1.0, 0.0).astype(BF16)


def run_select(owners, groups):
    return pl.pallas_call(
        functools.partial(select_kernel, groups),
        out_shape=jax.ShapeDtypeStruct((LANES, 2 * LANES), BF16),
        in_specs=[VM],
        out_specs=VM,
        name="select",
    )(owners.reshape(1, LANES))


def margin_kernel(groups, recv_ref, coef_ref, scale_ref, slab_ref, out_ref, rows_ref):
    for g in range(groups):
        for s in range(CAP):
            block = recv_ref[g, s * CHUNKS : (s + 1) * CHUNKS, :].astype(F32)
            row = (s * (groups // 8) + g // 8) * (8 * CHUNKS) + g % 8 * 8
            for q in range(CHUNKS // 8):
                rows_ref[pl.ds(row + q * 64, 8), :] = block[q * 8 : q * 8 + 8]

    def column(c):
        start = c // 8 * 64 + c % 8
        tiles = [
            rows_ref[pl.ds(start + t * 8 * CHUNKS, 8, stride=8), :] for t in range(CAP * groups // 8)
        ]
        return jnp.concatenate(tiles, axis=0)

    acc = jnp.zeros((CAP * groups, LANES), F32)
    for i in range(SIDE):
        lhs = jnp.concatenate([column(2 * i), column(2 * i + 1)], axis=1).astype(BF16)
        acc = acc + mm(lhs, coef_ref[i * PLANE : (i + 1) * PLANE, :])
    acc = acc * (scale_ref[...] * (1.0 / float(SIDE) ** 1.5))
    for s in range(CAP):
        out_ref[pl.ds(s, groups, stride=BACK), :] = acc[s * groups : (s + 1) * groups]
    slab = slab_ref[...]
    for h in range(2):
        out_ref[pl.ds(CAP + h, groups, stride=BACK), :] = jnp.broadcast_to(
            slab[:, h * LANES : (h + 1) * LANES], (groups, LANES)
        )


def run_margin(received, owned, kernel_diag, slab, groups):
    return pl.pallas_call(
        functools.partial(margin_kernel, groups),
        out_shape=jax.ShapeDtypeStruct((groups * BACK, LANES), F32),
        in_specs=[VM, VM, VM, VM],
        out_specs=VM,
        scratch_shapes=[pltpu.VMEM((CAP * groups * CHUNKS, LANES), F32)],
        compiler_params=pltpu.CompilerParams(vmem_limit_bytes=16 * 1024 * 1024),
        name="margin",
    )(received, owned, kernel_diag.reshape(1, LANES), slab)


def gather_kernel(groups, select_ref, ret_hbm, out_ref, dens_ref, ret_ref, sem):
    copy = pltpu.make_async_copy(ret_hbm, ret_ref, sem)
    copy.start()
    copy.wait()
    rows = [ret_ref[pl.ds(s, groups, stride=BACK), :] for s in range(CAP + 2)]
    x = jnp.concatenate(rows[:CAP] + [jnp.zeros((groups, LANES), F32)], axis=0)
    hi, mid = split2(x)
    lo = (x - hi.astype(F32) - mid.astype(F32)).astype(BF16)
    y = mm(select_ref[...], jnp.concatenate([hi, mid], axis=1))
    out_ref[...] = y[:, :LANES] + (y[:, LANES:] + mm(select_ref[...], lo))
    for h in range(2):
        dens_ref[:, h * LANES : (h + 1) * LANES] = jnp.sum(
            rows[CAP + h].reshape(groups // HALF, HALF, LANES), axis=0
        )


def run_gather(select, returned, groups):
    return pl.pallas_call(
        functools.partial(gather_kernel, groups),
        out_shape=(
            jax.ShapeDtypeStruct((LANES, LANES), F32),
            jax.ShapeDtypeStruct((HALF, PLANE), F32),
        ),
        in_specs=[VM, HBM],
        out_specs=(VM, VM),
        scratch_shapes=[
            pltpu.VMEM((groups * BACK, LANES), F32),
            pltpu.SemaphoreType.DMA,
        ],
        compiler_params=pltpu.CompilerParams(vmem_limit_bytes=4 * 1024 * 1024),
        name="gather",
    )(select, returned)


def body(support, potential, magic_taps, kinetic_taps, kernel_diag, owners):
    groups = lax.axis_size("grp")
    domains = lax.axis_size("dom")
    outgoing, part = run_apply(support, potential, magic_taps, kinetic_taps, kernel_diag, owners, groups)
    received = lax.all_to_all(outgoing, "grp", split_axis=0, concat_axis=0, tiled=True)
    owners_late, support_late, part = lax.optimization_barrier((owners, support, part))
    select = run_select(owners_late, groups)
    owned = support_late.reshape(CELLS, LANES).astype(BF16)
    distance = 1
    while distance < HALF:
        part = part + lax.ppermute(part, "grp", [(i, i ^ distance) for i in range(groups)])
        distance *= 2
    upper = lax.ppermute(part[HALF:], "dom", [(i, (i + 1) % domains) for i in range(domains)])
    mine = lax.axis_index("grp") % HALF
    slab = lax.dynamic_slice_in_dim(part[:HALF] + upper, mine, 1, 0)
    slab, select = lax.optimization_barrier((slab, select))
    products = run_margin(received, owned, kernel_diag, slab, groups)
    returned = lax.all_to_all(
        products.reshape(groups, BACK, 1, LANES), "grp", split_axis=0, concat_axis=0, tiled=True
    )
    return run_gather(select, returned.reshape(groups * BACK, LANES), groups)


def solution(mesh):
    return jax.shard_map(
        body,
        mesh=mesh,
        in_specs=(
            P(None, None, None, ("dom", "grp")),
            P(None, None, None, ("dom", "grp")),
            P(),
            P(),
            P(("dom", "grp")),
            P(("dom", "grp"), None),
        ),
        out_specs=(P(("dom", "grp"), None), P("dom", None)),
        check_vma=False,
    )
```

```python
import functools

import jax
import jax.numpy as jnp
from jax import lax
from jax.experimental import pallas as pl
from jax.experimental.pallas import tpu as pltpu
from jax.sharding import PartitionSpec as P

F32 = jnp.float32
BF16 = jnp.bfloat16
SIDE = 16
HALF = SIDE // 2
PLANE = SIDE * SIDE
CELLS = SIDE**3
LANES = 128
CAP = 3
CHUNKS = CELLS // LANES
BLOCK = CAP * CHUNKS
BACK = CAP + 2
NT = (((1,), (1,)), ((), ()))

VM = pl.BlockSpec(memory_space=pltpu.VMEM)
HBM = pl.BlockSpec(memory_space=pltpu.HBM)


def split2(x):
    hi = x.astype(BF16)
    lo = (x - hi.astype(F32)).astype(BF16)
    return hi, lo


def mm(a, b):
    return jnp.dot(a, b, preferred_element_type=F32)


def tap_lookup(taps_ref, offset):
    out = jnp.zeros(offset.shape, F32)
    for q in range(SIDE):
        out = jnp.where(offset == q, taps_ref[q], out)
    return out


def stack3(x):
    hi, lo = split2(x)
    return jnp.concatenate([hi, hi, lo], axis=0)


def slot_of(owner_row):
    n = owner_row.shape[1]
    across = jnp.broadcast_to(owner_row.astype(F32), (n, n))
    down = across.T
    r = lax.broadcasted_iota(jnp.int32, (n, n), 0)
    c = lax.broadcasted_iota(jnp.int32, (n, n), 1)
    earlier = jnp.where((across == down) & (r < c), 1.0, 0.0)
    return jnp.sum(earlier, axis=0, keepdims=True).astype(jnp.int32)


def plane_patterns(taps, flip):
    half = SIDE // 2 - 1
    a = lax.broadcasted_iota(jnp.int32, (SIDE, PLANE), 0)
    c = lax.broadcasted_iota(jnp.int32, (SIDE, PLANE), 1)
    minor = jnp.bitwise_and(c, SIDE - 1) - a
    major = jnp.right_shift(c, 4) - a
    if flip:
        minor, major = -minor, -major
    return tap_lookup(taps, minor + half), tap_lookup(taps, major + half)


def put_split(dst, row, mat, third):
    hi, lo = split2(mat)
    dst[row : row + SIDE, 0:PLANE] = hi
    dst[row : row + SIDE, PLANE : 2 * PLANE] = lo
    if third:
        dst[row : row + SIDE, 2 * PLANE : 3 * PLANE] = hi


def build_first(magic, kinetic, lhs1):
    f_minor, f_major = plane_patterns(magic, False)
    k_minor, k_major = plane_patterns(kinetic, False)
    a = lax.broadcasted_iota(jnp.int32, (SIDE, PLANE), 0)
    c = lax.broadcasted_iota(jnp.int32, (SIDE, PLANE), 1)
    same_minor = jnp.bitwise_and(c, SIDE - 1) == a
    lane_major = jnp.right_shift(c, 4)
    for g in range(SIDE):
        put_split(lhs1, g * SIDE, f_major[g : g + 1] * f_minor, False)
        kin = jnp.where(same_minor, k_major[g : g + 1], 0.0) + jnp.where(lane_major == g, k_minor, 0.0)
        put_split(lhs1, g * SIDE + PLANE, kin, False)


def build_last(magic, lhs_b):
    minor, major = plane_patterns(magic, True)
    for g in range(SIDE):
        put_split(lhs_b, g * SIDE, major[g : g + 1] * minor, True)


def build_side_matrix(taps, lhs, transposed, double):
    n = SIDE * HALF
    half = SIDE // 2 - 1
    a = lax.broadcasted_iota(jnp.int32, (SIDE, n), 0)
    c = lax.broadcasted_iota(jnp.int32, (SIDE, n), 1)
    delta = jnp.right_shift(c, 3) - a
    pattern = tap_lookup(taps, half - delta if transposed else delta + half)
    sub = lax.broadcasted_iota(jnp.int32, (HALF, n), 0)
    lane = lax.broadcasted_iota(jnp.int32, (HALF, n), 1)
    same = sub == jnp.bitwise_and(lane, HALF - 1)
    full = jnp.concatenate([jnp.where(same, pattern[i : i + 1], 0.0) for i in range(SIDE)], axis=0)
    hi, lo = split2(full)
    lhs[0:n, 0:n] = hi
    if not double:
        lhs[0:n, n : 2 * n] = lo
        return
    lhs[0:n, n : 2 * n] = hi
    lhs[n : 2 * n, 0:n] = lo
    lhs[n : 2 * n, n : 2 * n] = lo


def apply_kernel(
    groups,
    magic_hbm, kinetic_hbm, diag_hbm, owner_hbm, x_hbm, pot_hbm,
    out_hbm, dens_ref,
    x_ref, pot_ref, z_ref, kin_ref, kin_i_ref, r_ref, v_ref,
    lhs1, lhs_b, lhs_f, lhs_ft, lhs_k, sel_ref, rows_ref, stage_ref, grad_ref,
    magic, kinetic, diag_ref, owner_ref,
    sem_s, sem_x, sem_p, sem_o,
):
    small = [
        pltpu.make_async_copy(src, dst, sem_s.at[q])
        for q, (src, dst) in enumerate(
            [(magic_hbm, magic), (kinetic_hbm, kinetic), (diag_hbm, diag_ref), (owner_hbm, owner_ref)]
        )
    ]
    parts = 4
    width = SIDE // parts
    copies_x, copies_p = [], []
    for q in range(parts):
        part = pl.ds(q * width, width)
        copies_x.append(pltpu.make_async_copy(x_hbm.at[part], x_ref.at[part], sem_x.at[q]))
        copies_p.append(pltpu.make_async_copy(pot_hbm.at[part], pot_ref.at[part], sem_p.at[q]))
    for c in small + copies_x + copies_p:
        c.start()
    for c in small:
        c.wait()

    build_first(magic, kinetic, lhs1)

    def planes(ref, p):
        a, b = ref[2 * p], ref[2 * p + 1]
        return jnp.concatenate([a.reshape(PLANE, LANES), b.reshape(PLANE, LANES)], axis=1)

    def phase_a(p, carry):
        x = planes(x_ref, p).astype(BF16)
        y = mm(lhs1[...], jnp.concatenate([x, x], axis=0))
        for h in (0, 1):
            cols = slice(h * LANES, (h + 1) * LANES)
            z_ref[2 * p + h] = y[:PLANE, cols].reshape(SIDE, SIDE, LANES)
            kin_ref[2 * p + h] = y[PLANE:, cols].reshape(SIDE, SIDE, LANES)
        return carry

    for c in copies_x:
        c.wait()
    for p in range(SIDE // 2):
        phase_a(p, 0)
        if p == 1:
            build_side_matrix(magic, lhs_f, False, True)
        if p == 2:
            build_side_matrix(magic, lhs_ft, True, True)
        if p == 3:
            build_side_matrix(kinetic, lhs_k, False, False)
        if p == 4:
            build_last(magic, lhs_b)
        if p == 5:
            owner = owner_ref[...]
            column = slot_of(owner) * groups + owner
            ri = lax.broadcasted_iota(jnp.int32, (CAP * groups, LANES), 0)
            sel_ref[...] = jnp.where(ri == column, 1.0, 0.0).astype(BF16)
    for c in copies_p:
        c.wait()

    side = SIDE * HALF
    diag = diag_ref[...] * (1.0 / (LANES * groups))
    diag2 = jnp.concatenate([diag, diag], axis=1)
    lane = lax.broadcasted_iota(jnp.int32, (HALF, LANES), 1)
    sub = lax.broadcasted_iota(jnp.int32, (HALF, LANES), 0)

    def column_pair(ref, j):
        s = ref[:, j]
        return jnp.concatenate(
            [s[:, :HALF].reshape(side, LANES), s[:, HALF:].reshape(side, LANES)], axis=1
        )

    def along_i(lhs, x):
        hi, lo = split2(x)
        y = mm(lhs[...], jnp.concatenate([hi, lo], axis=0))
        return y[:side] + y[side:]

    def filter_out(j):
        r_ref[j] = along_i(lhs_f, column_pair(z_ref, j))
        x = column_pair(x_ref, j).astype(BF16)
        kin_i_ref[j] = mm(lhs_k[...], jnp.concatenate([x, x], axis=0))

    def filter_back(j, total):
        r = r_ref[j]
        v_ref[j] = along_i(lhs_ft, r * column_pair(pot_ref, j))
        weighted = diag2 * r * r
        for h in (0, 1):
            here = lane == sub + (jnp.bitwise_and(j, HALF - 1) * SIDE + h * HALF)
            d = jnp.sum(weighted[:, h * LANES : (h + 1) * LANES], axis=1, keepdims=True)
            d = jnp.broadcast_to(d, (side, LANES)).reshape(SIDE, HALF, LANES)
            total = total + jnp.where(here[None], d, 0.0)
        return total

    for j in range(3):
        filter_out(j)
    total = jnp.zeros((SIDE, HALF, LANES), F32)
    for j in range(SIDE):
        if j + 3 < SIDE:
            filter_out(j + 3)
        total = filter_back(j, total)
        if j % HALF == HALF - 1:
            t = j // HALF
            dens_ref[:, t * LANES : (t + 1) * LANES] = jnp.sum(total, axis=1)
            total = jnp.zeros((SIDE, HALF, LANES), F32)

    def slab_planes(ref, p):
        def one(i):
            rows = pl.ds(i * HALF, HALF)
            both = [ref[:, rows, h * LANES : (h + 1) * LANES] for h in (0, 1)]
            return jnp.concatenate(both, axis=1).reshape(PLANE, LANES)

        return jnp.concatenate([one(2 * p), one(2 * p + 1)], axis=1)

    def gradient(p):
        g = mm(lhs_b[...], stack3(slab_planes(v_ref, p))) + (planes(kin_ref, p) + slab_planes(kin_i_ref, p))
        grad_ref[p] = g.astype(BF16)

    def dispatch(p):
        for h in (0, 1):
            sent = lax.dot_general(
                sel_ref[...], grad_ref[p, :, h * LANES : (h + 1) * LANES], NT, preferred_element_type=F32
            )
            for c in (0, 1):
                chunk = 4 * p + 2 * h + c
                place = chunk // 8 * 64 + chunk % 8
                for t in range(CAP * groups // 8):
                    rows_ref[pl.ds(place + t * 8 * CHUNKS, 8, stride=8), :] = sent[
                        t * 8 : t * 8 + 8, c * LANES : (c + 1) * LANES
                    ]

    def pack(g, half):
        tile, within = g // 8, g % 8
        for s in range(CAP):
            row = (s * (groups // 8) + tile) * (8 * CHUNKS) + within * 8
            parts = [rows_ref[pl.ds(row + q * 64, 8), :] for q in (2 * half, 2 * half + 1)]
            at = s * CHUNKS + half * CHUNKS // 2
            stage_ref[g, at : at + CHUNKS // 2, :] = jnp.concatenate(parts, axis=0).astype(BF16)

    bands = 4
    per = groups // bands
    steps = SIDE // 2
    gradient(0)
    for p in range(1, steps + 1):
        if p < steps:
            gradient(p)
        dispatch(p - 1)
        if p > steps // 2:
            for g in range((p - 1 - steps // 2) * per, (p - steps // 2) * per):
                pack(g, 0)

    outs = []
    for b in range(bands):
        for g in range(b * per, (b + 1) * per):
            pack(g, 1)
        part = pl.ds(b * per, per)
        outs.append(pltpu.make_async_copy(stage_ref.at[part], out_hbm.at[part], sem_o.at[b]))
        outs[-1].start()
    for c in outs:
        c.wait()


def run_apply(support, potential, magic_taps, kinetic_taps, kernel_diag, owners, groups):
    box = pltpu.VMEM((SIDE, SIDE, SIDE, LANES), F32)
    side = SIDE * HALF
    slab = pltpu.VMEM((SIDE, side, 2 * LANES), F32)
    side_lhs = pltpu.VMEM((2 * side, 2 * side), BF16)
    dma = pltpu.SemaphoreType.DMA((4,))
    return pl.pallas_call(
        functools.partial(apply_kernel, groups),
        out_shape=(
            jax.ShapeDtypeStruct((groups, BLOCK, LANES), BF16),
            jax.ShapeDtypeStruct((SIDE, PLANE), F32),
        ),
        in_specs=[HBM] * 6,
        out_specs=(HBM, VM),
        scratch_shapes=[
            box, box, box, box, slab, slab, slab,
            pltpu.VMEM((2 * PLANE, 2 * PLANE), BF16),
            pltpu.VMEM((PLANE, 3 * PLANE), BF16),
            side_lhs, side_lhs,
            pltpu.VMEM((side, 2 * side), BF16),
            pltpu.VMEM((CAP * groups, LANES), BF16),
            pltpu.VMEM((CAP * groups * CHUNKS, LANES), F32),
            pltpu.VMEM((groups, BLOCK, LANES), BF16),
            pltpu.VMEM((SIDE // 2, PLANE, 2 * LANES), BF16),
            pltpu.SMEM((SIDE,), F32), pltpu.SMEM((SIDE,), F32),
            pltpu.VMEM((1, LANES), F32), pltpu.VMEM((1, LANES), jnp.int32),
            dma, dma, dma, dma,
        ],
        compiler_params=pltpu.CompilerParams(vmem_limit_bytes=48 * 1024 * 1024),
        name="apply",
    )(*[
        pltpu.with_memory_space_constraint(v, pltpu.HBM)
        for v in (magic_taps, kinetic_taps, kernel_diag.reshape(1, LANES), owners.reshape(1, LANES), support, potential)
    ])


def select_kernel(groups, owner_ref, out_ref):
    owner = owner_ref[...]
    column = slot_of(owner) * groups + owner
    down = jnp.broadcast_to(column.astype(F32), (LANES, LANES)).T
    lane = lax.broadcasted_iota(jnp.int32, (LANES, LANES), 1).astype(F32)
    for t in range(CAP * groups // LANES + 1):
        out_ref[:, t * LANES : (t + 1) * LANES] = jnp.where(down == lane + float(t * LANES), 1.0, 0.0).astype(BF16)


def run_select(owners, groups):
    return pl.pallas_call(
        functools.partial(select_kernel, groups),
        out_shape=jax.ShapeDtypeStruct((LANES, 2 * LANES), BF16),
        in_specs=[VM],
        out_specs=VM,
        name="select",
    )(owners.reshape(1, LANES))


def margin_kernel(groups, recv_ref, coef_ref, scale_ref, slab_ref, out_ref, rows_ref):
    for g in range(groups):
        for s in range(CAP):
            block = recv_ref[g, s * CHUNKS : (s + 1) * CHUNKS, :].astype(F32)
            row = (s * (groups // 8) + g // 8) * (8 * CHUNKS) + g % 8 * 8
            for q in range(CHUNKS // 8):
                rows_ref[pl.ds(row + q * 64, 8), :] = block[q * 8 : q * 8 + 8]

    def column(c):
        start = c // 8 * 64 + c % 8
        tiles = [
            rows_ref[pl.ds(start + t * 8 * CHUNKS, 8, stride=8), :] for t in range(CAP * groups // 8)
        ]
        return jnp.concatenate(tiles, axis=0)

    acc = jnp.zeros((CAP * groups, LANES), F32)
    for i in range(SIDE):
        lhs = jnp.concatenate([column(2 * i), column(2 * i + 1)], axis=1).astype(BF16)
        acc = acc + mm(lhs, coef_ref[i * PLANE : (i + 1) * PLANE, :])
    acc = acc * (scale_ref[...] * (1.0 / float(SIDE) ** 1.5))
    for s in range(CAP):
        out_ref[pl.ds(s, groups, stride=BACK), :] = acc[s * groups : (s + 1) * groups]
    slab = slab_ref[...]
    for h in range(2):
        out_ref[pl.ds(CAP + h, groups, stride=BACK), :] = jnp.broadcast_to(
            slab[:, h * LANES : (h + 1) * LANES], (groups, LANES)
        )


def run_margin(received, owned, kernel_diag, slab, groups):
    return pl.pallas_call(
        functools.partial(margin_kernel, groups),
        out_shape=jax.ShapeDtypeStruct((groups * BACK, LANES), F32),
        in_specs=[VM, VM, VM, VM],
        out_specs=VM,
        scratch_shapes=[pltpu.VMEM((CAP * groups * CHUNKS, LANES), F32)],
        compiler_params=pltpu.CompilerParams(vmem_limit_bytes=16 * 1024 * 1024),
        name="margin",
    )(received, owned, kernel_diag.reshape(1, LANES), slab)


def gather_kernel(groups, select_ref, ret_hbm, out_ref, dens_ref, ret_ref, sem):
    copy = pltpu.make_async_copy(ret_hbm, ret_ref, sem)
    copy.start()
    copy.wait()
    rows = [ret_ref[pl.ds(s, groups, stride=BACK), :] for s in range(CAP + 2)]
    x = jnp.concatenate(rows[:CAP] + [jnp.zeros((groups, LANES), F32)], axis=0)
    hi, mid = split2(x)
    lo = (x - hi.astype(F32) - mid.astype(F32)).astype(BF16)
    y = mm(select_ref[...], jnp.concatenate([hi, mid], axis=1))
    out_ref[...] = y[:, :LANES] + (y[:, LANES:] + mm(select_ref[...], lo))
    for h in range(2):
        dens_ref[:, h * LANES : (h + 1) * LANES] = jnp.sum(
            rows[CAP + h].reshape(groups // HALF, HALF, LANES), axis=0
        )


def run_gather(select, returned, groups):
    return pl.pallas_call(
        functools.partial(gather_kernel, groups),
        out_shape=(
            jax.ShapeDtypeStruct((LANES, LANES), F32),
            jax.ShapeDtypeStruct((HALF, PLANE), F32),
        ),
        in_specs=[VM, HBM],
        out_specs=(VM, VM),
        scratch_shapes=[
            pltpu.VMEM((groups * BACK, LANES), F32),
            pltpu.SemaphoreType.DMA,
        ],
        compiler_params=pltpu.CompilerParams(vmem_limit_bytes=4 * 1024 * 1024),
        name="gather",
    )(select, returned)


def body(support, potential, magic_taps, kinetic_taps, kernel_diag, owners):
    groups = lax.axis_size("grp")
    domains = lax.axis_size("dom")
    outgoing, part = run_apply(support, potential, magic_taps, kinetic_taps, kernel_diag, owners, groups)
    received = lax.all_to_all(outgoing, "grp", split_axis=0, concat_axis=0, tiled=True)
    owners_late, support_late, part = lax.optimization_barrier((owners, support, part))
    select = run_select(owners_late, groups)
    owned = support_late.reshape(CELLS, LANES).astype(BF16)
    distance = 1
    while distance < HALF:
        part = part + lax.ppermute(part, "grp", [(i, i ^ distance) for i in range(groups)])
        distance *= 2
    upper = lax.ppermute(part[HALF:], "dom", [(i, (i + 1) % domains) for i in range(domains)])
    mine = lax.axis_index("grp") % HALF
    slab = lax.dynamic_slice_in_dim(part[:HALF] + upper, mine, 1, 0)
    slab, select = lax.optimization_barrier((slab, select))
    products = run_margin(received, owned, kernel_diag, slab, groups)
    returned = lax.all_to_all(
        products.reshape(groups, BACK, 1, LANES), "grp", split_axis=0, concat_axis=0, tiled=True
    )
    return run_gather(select, returned.reshape(groups * BACK, LANES), groups)


def solution(mesh):
    return jax.shard_map(
        body,
        mesh=mesh,
        in_specs=(
            P(None, None, None, ("dom", "grp")),
            P(None, None, None, ("dom", "grp")),
            P(),
            P(),
            P(("dom", "grp")),
            P(("dom", "grp"), None),
        ),
        out_specs=(P(("dom", "grp"), None), P("dom", None)),
        check_vma=False,
    )
```

```python
import functools

import jax
import jax.numpy as jnp
from jax import lax
from jax.experimental import pallas as pl
from jax.experimental.pallas import tpu as pltpu
from jax.sharding import PartitionSpec as P

F32 = jnp.float32
BF16 = jnp.bfloat16
SIDE = 16
HALF = SIDE // 2
PLANE = SIDE * SIDE
CELLS = SIDE**3
LANES = 128
CAP = 3
CHUNKS = CELLS // LANES
BLOCK = CAP * CHUNKS
BACK = CAP + 3
NT = (((1,), (1,)), ((), ()))

VM = pl.BlockSpec(memory_space=pltpu.VMEM)
HBM = pl.BlockSpec(memory_space=pltpu.HBM)


def split2(x):
    hi = x.astype(BF16)
    lo = (x - hi.astype(F32)).astype(BF16)
    return hi, lo


def mm(a, b):
    return jnp.dot(a, b, preferred_element_type=F32)


def tap_lookup(taps_ref, offset):
    out = jnp.zeros(offset.shape, F32)
    for q in range(SIDE):
        out = jnp.where(offset == q, taps_ref[q], out)
    return out


def stack3(x):
    hi, lo = split2(x)
    return jnp.concatenate([hi, hi, lo], axis=0)


def slot_of(owner_row):
    n = owner_row.shape[1]
    across = jnp.broadcast_to(owner_row.astype(F32), (n, n))
    down = across.T
    r = lax.broadcasted_iota(jnp.int32, (n, n), 0)
    c = lax.broadcasted_iota(jnp.int32, (n, n), 1)
    earlier = jnp.where((across == down) & (r < c), 1.0, 0.0)
    return jnp.sum(earlier, axis=0, keepdims=True).astype(jnp.int32)


def plane_patterns(taps, flip):
    half = SIDE // 2 - 1
    a = lax.broadcasted_iota(jnp.int32, (SIDE, PLANE), 0)
    c = lax.broadcasted_iota(jnp.int32, (SIDE, PLANE), 1)
    minor = jnp.bitwise_and(c, SIDE - 1) - a
    major = jnp.right_shift(c, 4) - a
    if flip:
        minor, major = -minor, -major
    return tap_lookup(taps, minor + half), tap_lookup(taps, major + half)


def put_split(dst, row, mat, third):
    hi, lo = split2(mat)
    if not third:
        dst[row : row + SIDE, :] = hi
        dst[row + 2 * PLANE : row + 2 * PLANE + SIDE, :] = lo
        return
    dst[row : row + SIDE, 0:PLANE] = hi
    dst[row : row + SIDE, PLANE : 2 * PLANE] = lo
    dst[row : row + SIDE, 2 * PLANE : 3 * PLANE] = hi


def build_first(magic, kinetic, lhs1):
    f_minor, f_major = plane_patterns(magic, False)
    k_minor, k_major = plane_patterns(kinetic, False)
    a = lax.broadcasted_iota(jnp.int32, (SIDE, PLANE), 0)
    c = lax.broadcasted_iota(jnp.int32, (SIDE, PLANE), 1)
    same_minor = jnp.bitwise_and(c, SIDE - 1) == a
    lane_major = jnp.right_shift(c, 4)
    for g in range(SIDE):
        put_split(lhs1, g * SIDE, f_major[g : g + 1] * f_minor, False)
        kin = jnp.where(same_minor, k_major[g : g + 1], 0.0) + jnp.where(lane_major == g, k_minor, 0.0)
        put_split(lhs1, g * SIDE + PLANE, kin, False)


def build_last(magic, lhs_b):
    minor, major = plane_patterns(magic, True)
    for g in range(SIDE):
        put_split(lhs_b, g * SIDE, major[g : g + 1] * minor, True)


def build_side_matrix(taps, lhs, transposed, double):
    n = SIDE * HALF
    half = SIDE // 2 - 1
    a = lax.broadcasted_iota(jnp.int32, (SIDE, n), 0)
    c = lax.broadcasted_iota(jnp.int32, (SIDE, n), 1)
    delta = jnp.right_shift(c, 3) - a
    pattern = tap_lookup(taps, half - delta if transposed else delta + half)
    sub = lax.broadcasted_iota(jnp.int32, (HALF, n), 0)
    lane = lax.broadcasted_iota(jnp.int32, (HALF, n), 1)
    same = sub == jnp.bitwise_and(lane, HALF - 1)
    full = jnp.concatenate([jnp.where(same, pattern[i : i + 1], 0.0) for i in range(SIDE)], axis=0)
    hi, lo = split2(full)
    lhs[0:n, 0:n] = hi
    if not double:
        lhs[0:n, n : 2 * n] = lo
        return
    lhs[0:n, n : 2 * n] = hi
    lhs[n : 2 * n, 0:n] = lo
    lhs[n : 2 * n, n : 2 * n] = lo


def apply_kernel(
    groups,
    magic_hbm, kinetic_hbm, diag_hbm, owner_hbm, x_hbm, pot_hbm,
    out_hbm, dens_ref,
    x_ref, pot_ref, z_ref, kin_ref, kin_i_ref, r_ref, v_ref,
    lhs1, lhs_b, lhs_f, lhs_ft, lhs_k, sel_ref, rows_ref, stage_ref, grad_ref,
    magic, kinetic, diag_ref, owner_ref,
    sem_s, sem_x, sem_p, sem_o,
):
    small = [
        pltpu.make_async_copy(src, dst, sem_s.at[q])
        for q, (src, dst) in enumerate(
            [(magic_hbm, magic), (kinetic_hbm, kinetic), (diag_hbm, diag_ref), (owner_hbm, owner_ref)]
        )
    ]
    parts = 4
    width = SIDE // parts
    copies_x, copies_p = [], []
    for q in range(parts):
        part = pl.ds(q * width, width)
        copies_x.append(pltpu.make_async_copy(x_hbm.at[part], x_ref.at[part], sem_x.at[q]))
        copies_p.append(pltpu.make_async_copy(pot_hbm.at[part], pot_ref.at[part], sem_p.at[q]))
    for c in small + copies_x + copies_p:
        c.start()
    for c in small:
        c.wait()

    build_first(magic, kinetic, lhs1)

    def planes(ref, p):
        a, b = ref[2 * p], ref[2 * p + 1]
        return jnp.concatenate([a.reshape(PLANE, LANES), b.reshape(PLANE, LANES)], axis=1)

    def phase_a(p, carry):
        y = mm(lhs1[...], planes(x_ref, p).astype(BF16))
        y = y[: 2 * PLANE] + y[2 * PLANE :]
        for h in (0, 1):
            cols = slice(h * LANES, (h + 1) * LANES)
            z_ref[2 * p + h] = y[:PLANE, cols].reshape(SIDE, SIDE, LANES)
            kin_ref[2 * p + h] = y[PLANE:, cols].reshape(SIDE, SIDE, LANES)
        return carry

    for c in copies_x:
        c.wait()
    for p in range(SIDE // 2):
        phase_a(p, 0)
        if p == 1:
            build_side_matrix(magic, lhs_f, False, True)
        if p == 2:
            build_side_matrix(magic, lhs_ft, True, True)
        if p == 3:
            build_side_matrix(kinetic, lhs_k, False, False)
        if p == 4:
            build_last(magic, lhs_b)
        if p == 5:
            owner = owner_ref[...]
            column = slot_of(owner) * groups + owner
            ri = lax.broadcasted_iota(jnp.int32, (CAP * groups, LANES), 0)
            sel_ref[...] = jnp.where(ri == column, 1.0, 0.0).astype(BF16)
    for c in copies_p:
        c.wait()

    side = SIDE * HALF
    diag = diag_ref[...] * (1.0 / (LANES * groups))
    diag2 = jnp.concatenate([diag, diag], axis=1)
    lane = lax.broadcasted_iota(jnp.int32, (HALF, LANES), 1)
    sub = lax.broadcasted_iota(jnp.int32, (HALF, LANES), 0)

    def column_pair(ref, j):
        s = ref[:, j]
        return jnp.concatenate(
            [s[:, :HALF].reshape(side, LANES), s[:, HALF:].reshape(side, LANES)], axis=1
        )

    def along_i(lhs, x):
        hi, lo = split2(x)
        y = mm(lhs[...], jnp.concatenate([hi, lo], axis=0))
        return y[:side] + y[side:]

    def filter_out(j):
        r_ref[j] = along_i(lhs_f, column_pair(z_ref, j))
        x = column_pair(x_ref, j).astype(BF16)
        kin_i_ref[j] = mm(lhs_k[...], jnp.concatenate([x, x], axis=0))

    def filter_back(j, total):
        r = r_ref[j]
        v_ref[j] = along_i(lhs_ft, r * column_pair(pot_ref, j))
        weighted = diag2 * r * r
        for h in (0, 1):
            here = lane == sub + (jnp.bitwise_and(j, HALF - 1) * SIDE + h * HALF)
            d = jnp.sum(weighted[:, h * LANES : (h + 1) * LANES], axis=1, keepdims=True)
            d = jnp.broadcast_to(d, (side, LANES)).reshape(SIDE, HALF, LANES)
            total = total + jnp.where(here[None], d, 0.0)
        return total

    for j in range(3):
        filter_out(j)
    total = jnp.zeros((SIDE, HALF, LANES), F32)
    for j in range(SIDE):
        if j + 3 < SIDE:
            filter_out(j + 3)
        total = filter_back(j, total)
        if j % HALF == HALF - 1:
            t = j // HALF
            dens_ref[:, t * LANES : (t + 1) * LANES] = jnp.sum(total, axis=1)
            total = jnp.zeros((SIDE, HALF, LANES), F32)

    def slab_planes(ref, p):
        def one(i):
            rows = pl.ds(i * HALF, HALF)
            both = [ref[:, rows, h * LANES : (h + 1) * LANES] for h in (0, 1)]
            return jnp.concatenate(both, axis=1).reshape(PLANE, LANES)

        return jnp.concatenate([one(2 * p), one(2 * p + 1)], axis=1)

    def gradient(p):
        g = mm(lhs_b[...], stack3(slab_planes(v_ref, p))) + (planes(kin_ref, p) + slab_planes(kin_i_ref, p))
        grad_ref[p] = g.astype(BF16)

    def dispatch(p):
        for h in (0, 1):
            sent = lax.dot_general(
                sel_ref[...], grad_ref[p, :, h * LANES : (h + 1) * LANES], NT, preferred_element_type=F32
            )
            for c in (0, 1):
                chunk = 4 * p + 2 * h + c
                place = chunk // 8 * 64 + chunk % 8
                for t in range(CAP * groups // 8):
                    rows_ref[pl.ds(place + t * 8 * CHUNKS, 8, stride=8), :] = sent[
                        t * 8 : t * 8 + 8, c * LANES : (c + 1) * LANES
                    ]

    def pack(g, half):
        tile, within = g // 8, g % 8
        for s in range(CAP):
            row = (s * (groups // 8) + tile) * (8 * CHUNKS) + within * 8
            parts = [rows_ref[pl.ds(row + q * 64, 8), :] for q in (2 * half, 2 * half + 1)]
            at = s * CHUNKS + half * CHUNKS // 2
            stage_ref[g, at : at + CHUNKS // 2, :] = jnp.concatenate(parts, axis=0).astype(BF16)

    bands = 4
    per = groups // bands
    steps = SIDE // 2
    gradient(0)
    for p in range(1, steps + 1):
        if p < steps:
            gradient(p)
        dispatch(p - 1)
        if p > steps // 2:
            for g in range((p - 1 - steps // 2) * per, (p - steps // 2) * per):
                pack(g, 0)

    outs = []
    for b in range(bands):
        for g in range(b * per, (b + 1) * per):
            pack(g, 1)
        part = pl.ds(b * per, per)
        outs.append(pltpu.make_async_copy(stage_ref.at[part], out_hbm.at[part], sem_o.at[b]))
        outs[-1].start()
    for c in outs:
        c.wait()


def run_apply(support, potential, magic_taps, kinetic_taps, kernel_diag, owners, groups):
    box = pltpu.VMEM((SIDE, SIDE, SIDE, LANES), F32)
    side = SIDE * HALF
    slab = pltpu.VMEM((SIDE, side, 2 * LANES), F32)
    side_lhs = pltpu.VMEM((2 * side, 2 * side), BF16)
    dma = pltpu.SemaphoreType.DMA((4,))
    return pl.pallas_call(
        functools.partial(apply_kernel, groups),
        out_shape=(
            jax.ShapeDtypeStruct((groups, BLOCK, LANES), BF16),
            jax.ShapeDtypeStruct((SIDE, PLANE), F32),
        ),
        in_specs=[HBM] * 6,
        out_specs=(HBM, VM),
        scratch_shapes=[
            box, box, box, box, slab, slab, slab,
            pltpu.VMEM((4 * PLANE, PLANE), BF16),
            pltpu.VMEM((PLANE, 3 * PLANE), BF16),
            side_lhs, side_lhs,
            pltpu.VMEM((side, 2 * side), BF16),
            pltpu.VMEM((CAP * groups, LANES), BF16),
            pltpu.VMEM((CAP * groups * CHUNKS, LANES), F32),
            pltpu.VMEM((groups, BLOCK, LANES), BF16),
            pltpu.VMEM((SIDE // 2, PLANE, 2 * LANES), BF16),
            pltpu.SMEM((SIDE,), F32), pltpu.SMEM((SIDE,), F32),
            pltpu.VMEM((1, LANES), F32), pltpu.VMEM((1, LANES), jnp.int32),
            dma, dma, dma, dma,
        ],
        compiler_params=pltpu.CompilerParams(vmem_limit_bytes=48 * 1024 * 1024),
        name="apply",
    )(*[
        pltpu.with_memory_space_constraint(v, pltpu.HBM)
        for v in (magic_taps, kinetic_taps, kernel_diag.reshape(1, LANES), owners.reshape(1, LANES), support, potential)
    ])


def select_kernel(groups, owner_ref, out_ref):
    owner = owner_ref[...]
    column = slot_of(owner) * groups + owner
    down = jnp.broadcast_to(column.astype(F32), (LANES, LANES)).T
    lane = lax.broadcasted_iota(jnp.int32, (LANES, LANES), 1).astype(F32)
    for t in range(CAP * groups // LANES + 1):
        out_ref[:, t * LANES : (t + 1) * LANES] = jnp.where(down == lane + float(t * LANES), 1.0, 0.0).astype(BF16)


def run_select(owners, groups):
    return pl.pallas_call(
        functools.partial(select_kernel, groups),
        out_shape=jax.ShapeDtypeStruct((LANES, 2 * LANES), BF16),
        in_specs=[VM],
        out_specs=VM,
        name="select",
    )(owners.reshape(1, LANES))


def margin_kernel(groups, recv_ref, coef_ref, scale_ref, slab_ref, out_ref, rows_ref, back_ref):
    for g in range(groups):
        for s in range(CAP):
            block = recv_ref[g, s * CHUNKS : (s + 1) * CHUNKS, :].astype(F32)
            row = (s * (groups // 8) + g // 8) * (8 * CHUNKS) + g % 8 * 8
            for q in range(CHUNKS // 8):
                rows_ref[pl.ds(row + q * 64, 8), :] = block[q * 8 : q * 8 + 8]

    def column(c):
        start = c // 8 * 64 + c % 8
        tiles = [
            rows_ref[pl.ds(start + t * 8 * CHUNKS, 8, stride=8), :] for t in range(CAP * groups // 8)
        ]
        return jnp.concatenate(tiles, axis=0)

    acc = jnp.zeros((CAP * groups, LANES), F32)
    for i in range(SIDE):
        lhs = jnp.concatenate([column(2 * i), column(2 * i + 1)], axis=1).astype(BF16)
        acc = acc + mm(lhs, coef_ref[i * PLANE : (i + 1) * PLANE, :])
    acc = acc * (scale_ref[...] * (1.0 / float(SIDE) ** 1.5))
    for s in range(CAP):
        back_ref[pl.ds(s, groups, stride=BACK), :] = acc[s * groups : (s + 1) * groups]
    slab = slab_ref[...]
    for h in range(2):
        back_ref[pl.ds(CAP + h, groups, stride=BACK), :] = jnp.broadcast_to(
            slab[:, h * LANES : (h + 1) * LANES], (groups, LANES)
        )
    back_ref[pl.ds(CAP + 2, groups, stride=BACK), :] = jnp.zeros((groups, LANES), F32)
    out_ref[...] = back_ref[...].astype(BF16)


def run_margin(received, owned, kernel_diag, slab, groups):
    return pl.pallas_call(
        functools.partial(margin_kernel, groups),
        out_shape=jax.ShapeDtypeStruct((groups * BACK, LANES), BF16),
        in_specs=[VM, VM, VM, VM],
        out_specs=VM,
        scratch_shapes=[
            pltpu.VMEM((CAP * groups * CHUNKS, LANES), F32),
            pltpu.VMEM((groups * BACK, LANES), F32),
        ],
        compiler_params=pltpu.CompilerParams(vmem_limit_bytes=16 * 1024 * 1024),
        name="margin",
    )(received, owned, kernel_diag.reshape(1, LANES), slab)


def gather_kernel(groups, select_ref, ret_hbm, out_ref, dens_ref, ret_ref, back_ref, sem):
    copy = pltpu.make_async_copy(ret_hbm, ret_ref, sem)
    copy.start()
    copy.wait()
    back_ref[...] = ret_ref[...].astype(F32)
    rows = [back_ref[pl.ds(s, groups, stride=BACK), :] for s in range(CAP + 2)]
    x = jnp.concatenate(rows[:CAP] + [jnp.zeros((groups, LANES), F32)], axis=0)
    out_ref[...] = mm(select_ref[...], x.astype(BF16))
    for h in range(2):
        dens_ref[:, h * LANES : (h + 1) * LANES] = jnp.sum(
            rows[CAP + h].reshape(groups // HALF, HALF, LANES), axis=0
        )


def run_gather(select, returned, groups):
    return pl.pallas_call(
        functools.partial(gather_kernel, groups),
        out_shape=(
            jax.ShapeDtypeStruct((LANES, LANES), F32),
            jax.ShapeDtypeStruct((HALF, PLANE), F32),
        ),
        in_specs=[VM, HBM],
        out_specs=(VM, VM),
        scratch_shapes=[
            pltpu.VMEM((groups * BACK, LANES), BF16),
            pltpu.VMEM((groups * BACK, LANES), F32),
            pltpu.SemaphoreType.DMA,
        ],
        compiler_params=pltpu.CompilerParams(vmem_limit_bytes=4 * 1024 * 1024),
        name="gather",
    )(select, returned)


def body(support, potential, magic_taps, kinetic_taps, kernel_diag, owners):
    groups = lax.axis_size("grp")
    domains = lax.axis_size("dom")
    outgoing, part = run_apply(support, potential, magic_taps, kinetic_taps, kernel_diag, owners, groups)
    received = lax.all_to_all(outgoing, "grp", split_axis=0, concat_axis=0, tiled=True)
    owners_late, support_late, part = lax.optimization_barrier((owners, support, part))
    select = run_select(owners_late, groups)
    owned = support_late.reshape(CELLS, LANES).astype(BF16)
    distance = 1
    while distance < HALF:
        part = part + lax.ppermute(part, "grp", [(i, i ^ distance) for i in range(groups)])
        distance *= 2
    upper = lax.ppermute(part[HALF:], "dom", [(i, (i + 1) % domains) for i in range(domains)])
    mine = lax.axis_index("grp") % HALF
    slab = lax.dynamic_slice_in_dim(part[:HALF] + upper, mine, 1, 0)
    slab, select = lax.optimization_barrier((slab, select))
    products = run_margin(received, owned, kernel_diag, slab, groups)
    returned = lax.all_to_all(
        products.reshape(groups, BACK // 2, 2, LANES), "grp", split_axis=0, concat_axis=0, tiled=True
    )
    return run_gather(select, returned.reshape(groups * BACK, LANES), groups)


def solution(mesh):
    return jax.shard_map(
        body,
        mesh=mesh,
        in_specs=(
            P(None, None, None, ("dom", "grp")),
            P(None, None, None, ("dom", "grp")),
            P(),
            P(),
            P(("dom", "grp")),
            P(("dom", "grp"), None),
        ),
        out_specs=(P(("dom", "grp"), None), P("dom", None)),
        check_vma=False,
    )
```

```python
import functools

import jax
import jax.numpy as jnp
from jax import lax
from jax.experimental import pallas as pl
from jax.experimental.pallas import tpu as pltpu
from jax.sharding import PartitionSpec as P

F32 = jnp.float32
BF16 = jnp.bfloat16
SIDE = 16
HALF = SIDE // 2
PLANE = SIDE * SIDE
CELLS = SIDE**3
LANES = 128
CAP = 3
CHUNKS = CELLS // LANES
BLOCK = CAP * CHUNKS
BACK = CAP + 3
NT = (((1,), (1,)), ((), ()))

VM = pl.BlockSpec(memory_space=pltpu.VMEM)
HBM = pl.BlockSpec(memory_space=pltpu.HBM)


def split2(x):
    hi = x.astype(BF16)
    lo = (x - hi.astype(F32)).astype(BF16)
    return hi, lo


def mm(a, b):
    return jnp.dot(a, b, preferred_element_type=F32)


def tap_lookup(taps_ref, offset):
    out = jnp.zeros(offset.shape, F32)
    for q in range(SIDE):
        out = jnp.where(offset == q, taps_ref[q], out)
    return out


def stack3(x):
    hi, lo = split2(x)
    return jnp.concatenate([hi, hi, lo], axis=0)


def slot_of(owner_row):
    n = owner_row.shape[1]
    across = jnp.broadcast_to(owner_row.astype(F32), (n, n))
    down = across.T
    r = lax.broadcasted_iota(jnp.int32, (n, n), 0)
    c = lax.broadcasted_iota(jnp.int32, (n, n), 1)
    earlier = jnp.where((across == down) & (r < c), 1.0, 0.0)
    return jnp.sum(earlier, axis=0, keepdims=True).astype(jnp.int32)


def plane_patterns(taps, flip):
    half = SIDE // 2 - 1
    a = lax.broadcasted_iota(jnp.int32, (SIDE, PLANE), 0)
    c = lax.broadcasted_iota(jnp.int32, (SIDE, PLANE), 1)
    minor = jnp.bitwise_and(c, SIDE - 1) - a
    major = jnp.right_shift(c, 4) - a
    if flip:
        minor, major = -minor, -major
    return tap_lookup(taps, minor + half), tap_lookup(taps, major + half)


def put_split(dst, row, mat, third):
    hi, lo = split2(mat)
    if not third:
        dst[row : row + SIDE, :] = hi
        dst[row + 2 * PLANE : row + 2 * PLANE + SIDE, :] = lo
        return
    dst[row : row + SIDE, 0:PLANE] = hi
    dst[row : row + SIDE, PLANE : 2 * PLANE] = lo
    dst[row : row + SIDE, 2 * PLANE : 3 * PLANE] = hi


def build_first(magic, kinetic, lhs1):
    f_minor, f_major = plane_patterns(magic, False)
    k_minor, k_major = plane_patterns(kinetic, False)
    a = lax.broadcasted_iota(jnp.int32, (SIDE, PLANE), 0)
    c = lax.broadcasted_iota(jnp.int32, (SIDE, PLANE), 1)
    same_minor = jnp.bitwise_and(c, SIDE - 1) == a
    lane_major = jnp.right_shift(c, 4)
    for g in range(SIDE):
        put_split(lhs1, g * SIDE, f_major[g : g + 1] * f_minor, False)
        kin = jnp.where(same_minor, k_major[g : g + 1], 0.0) + jnp.where(lane_major == g, k_minor, 0.0)
        put_split(lhs1, g * SIDE + PLANE, kin, False)


def build_last(magic, lhs_b):
    minor, major = plane_patterns(magic, True)
    for g in range(SIDE):
        put_split(lhs_b, g * SIDE, major[g : g + 1] * minor, True)


def build_side_matrix(taps, lhs, transposed, double):
    n = SIDE * HALF
    half = SIDE // 2 - 1
    a = lax.broadcasted_iota(jnp.int32, (SIDE, n), 0)
    c = lax.broadcasted_iota(jnp.int32, (SIDE, n), 1)
    delta = jnp.right_shift(c, 3) - a
    pattern = tap_lookup(taps, half - delta if transposed else delta + half)
    sub = lax.broadcasted_iota(jnp.int32, (HALF, n), 0)
    lane = lax.broadcasted_iota(jnp.int32, (HALF, n), 1)
    same = sub == jnp.bitwise_and(lane, HALF - 1)
    full = jnp.concatenate([jnp.where(same, pattern[i : i + 1], 0.0) for i in range(SIDE)], axis=0)
    hi, lo = split2(full)
    lhs[0:n, 0:n] = hi
    if not double:
        lhs[0:n, n : 2 * n] = lo
        return
    lhs[0:n, n : 2 * n] = hi
    lhs[n : 2 * n, 0:n] = lo
    lhs[n : 2 * n, n : 2 * n] = lo


def apply_kernel(
    groups,
    magic_hbm, kinetic_hbm, diag_hbm, owner_hbm, x_hbm, pot_hbm,
    out_hbm, dens_ref,
    x_ref, pot_ref, z_ref, kin_ref, kin_i_ref, r_ref, v_ref,
    lhs1, lhs_b, lhs_f, lhs_ft, lhs_k, sel_ref, rows_ref, stage_ref, grad_ref,
    magic, kinetic, diag_ref, owner_ref,
    sem_s, sem_x, sem_p, sem_o,
):
    small = [
        pltpu.make_async_copy(src, dst, sem_s.at[q])
        for q, (src, dst) in enumerate(
            [(magic_hbm, magic), (kinetic_hbm, kinetic), (diag_hbm, diag_ref), (owner_hbm, owner_ref)]
        )
    ]
    parts = 4
    width = SIDE // parts
    copies_x, copies_p = [], []
    for q in range(parts):
        part = pl.ds(q * width, width)
        copies_x.append(pltpu.make_async_copy(x_hbm.at[part], x_ref.at[part], sem_x.at[q]))
        copies_p.append(pltpu.make_async_copy(pot_hbm.at[part], pot_ref.at[part], sem_p.at[q]))
    for c in small + copies_x + copies_p:
        c.start()
    for c in small:
        c.wait()

    build_first(magic, kinetic, lhs1)

    def planes(ref, p):
        a, b = ref[2 * p], ref[2 * p + 1]
        return jnp.concatenate([a.reshape(PLANE, LANES), b.reshape(PLANE, LANES)], axis=1)

    def phase_a(p, carry):
        y = mm(lhs1[...], planes(x_ref, p).astype(BF16))
        y = y[: 2 * PLANE] + y[2 * PLANE :]
        for h in (0, 1):
            cols = slice(h * LANES, (h + 1) * LANES)
            z_ref[2 * p + h] = y[:PLANE, cols].reshape(SIDE, SIDE, LANES)
            kin_ref[2 * p + h] = y[PLANE:, cols].reshape(SIDE, SIDE, LANES)
        return carry

    for c in copies_x:
        c.wait()
    for p in range(SIDE // 2):
        phase_a(p, 0)
        if p == 1:
            build_side_matrix(magic, lhs_f, False, True)
        if p == 2:
            build_side_matrix(magic, lhs_ft, True, True)
        if p == 3:
            build_side_matrix(kinetic, lhs_k, False, False)
        if p == 4:
            build_last(magic, lhs_b)
        if p == 5:
            owner = owner_ref[...]
            column = slot_of(owner) * groups + owner
            ri = lax.broadcasted_iota(jnp.int32, (CAP * groups, LANES), 0)
            sel_ref[...] = jnp.where(ri == column, 1.0, 0.0).astype(BF16)
    for c in copies_p:
        c.wait()

    side = SIDE * HALF
    diag = diag_ref[...] * (1.0 / (LANES * groups))
    diag2 = jnp.concatenate([diag, diag], axis=1)
    lane = lax.broadcasted_iota(jnp.int32, (HALF, LANES), 1)
    sub = lax.broadcasted_iota(jnp.int32, (HALF, LANES), 0)

    def column_pair(ref, j):
        s = ref[:, j]
        return jnp.concatenate(
            [s[:, :HALF].reshape(side, LANES), s[:, HALF:].reshape(side, LANES)], axis=1
        )

    def along_i(lhs, x):
        hi, lo = split2(x)
        y = mm(lhs[...], jnp.concatenate([hi, lo], axis=0))
        return y[:side] + y[side:]

    def filter_out(j):
        r_ref[j] = along_i(lhs_f, column_pair(z_ref, j))
        x = column_pair(x_ref, j).astype(BF16)
        kin_i_ref[j] = mm(lhs_k[...], jnp.concatenate([x, x], axis=0))

    def filter_back(j, total):
        r = r_ref[j]
        v_ref[j] = along_i(lhs_ft, r * column_pair(pot_ref, j))
        weighted = diag2 * r * r
        for h in (0, 1):
            here = lane == sub + (jnp.bitwise_and(j, HALF - 1) * SIDE + h * HALF)
            d = jnp.sum(weighted[:, h * LANES : (h + 1) * LANES], axis=1, keepdims=True)
            d = jnp.broadcast_to(d, (side, LANES)).reshape(SIDE, HALF, LANES)
            total = total + jnp.where(here[None], d, 0.0)
        return total

    for j in range(3):
        filter_out(j)
    total = jnp.zeros((SIDE, HALF, LANES), F32)
    for j in range(SIDE):
        if j + 3 < SIDE:
            filter_out(j + 3)
        total = filter_back(j, total)
        if j % HALF == HALF - 1:
            t = j // HALF
            dens_ref[:, t * LANES : (t + 1) * LANES] = jnp.sum(total, axis=1)
            total = jnp.zeros((SIDE, HALF, LANES), F32)

    def slab_planes(ref, p):
        def one(i):
            rows = pl.ds(i * HALF, HALF)
            both = [ref[:, rows, h * LANES : (h + 1) * LANES] for h in (0, 1)]
            return jnp.concatenate(both, axis=1).reshape(PLANE, LANES)

        return jnp.concatenate([one(2 * p), one(2 * p + 1)], axis=1)

    def gradient(p):
        g = mm(lhs_b[...], stack3(slab_planes(v_ref, p))) + (planes(kin_ref, p) + slab_planes(kin_i_ref, p))
        grad_ref[p] = g.astype(BF16)

    def dispatch(p):
        for h in (0, 1):
            sent = lax.dot_general(
                sel_ref[...], grad_ref[p, :, h * LANES : (h + 1) * LANES], NT, preferred_element_type=F32
            )
            for c in (0, 1):
                chunk = 4 * p + 2 * h + c
                place = chunk // 8 * 64 + chunk % 8
                for t in range(CAP * groups // 8):
                    rows_ref[pl.ds(place + t * 8 * CHUNKS, 8, stride=8), :] = sent[
                        t * 8 : t * 8 + 8, c * LANES : (c + 1) * LANES
                    ]

    def pack(g, half):
        tile, within = g // 8, g % 8
        for s in range(CAP):
            row = (s * (groups // 8) + tile) * (8 * CHUNKS) + within * 8
            parts = [rows_ref[pl.ds(row + q * 64, 8), :] for q in (2 * half, 2 * half + 1)]
            at = s * CHUNKS + half * CHUNKS // 2
            stage_ref[g, at : at + CHUNKS // 2, :] = jnp.concatenate(parts, axis=0).astype(BF16)

    bands = 4
    per = groups // bands
    steps = SIDE // 2
    outs = []

    def send(first, count, half):
        for s in range(CAP):
            part = (pl.ds(first, count), pl.ds(s * CHUNKS + half * CHUNKS // 2, CHUNKS // 2))
            outs.append(pltpu.make_async_copy(stage_ref.at[part], out_hbm.at[part], sem_o.at[len(outs)]))
            outs[-1].start()

    gradient(0)
    for p in range(1, steps + 1):
        if p < steps:
            gradient(p)
        dispatch(p - 1)
        if p > steps // 2:
            for g in range((p - 1 - steps // 2) * per, (p - steps // 2) * per):
                pack(g, 0)
        if p == steps - 1:
            send(0, 3 * per, 0)
    send(3 * per, per, 0)

    for b in range(bands):
        for g in range(b * per, (b + 1) * per):
            pack(g, 1)
        send(b * per, per, 1)
    for c in outs:
        c.wait()


def run_apply(support, potential, magic_taps, kinetic_taps, kernel_diag, owners, groups):
    box = pltpu.VMEM((SIDE, SIDE, SIDE, LANES), F32)
    side = SIDE * HALF
    slab = pltpu.VMEM((SIDE, side, 2 * LANES), F32)
    side_lhs = pltpu.VMEM((2 * side, 2 * side), BF16)
    dma = pltpu.SemaphoreType.DMA((4,))
    return pl.pallas_call(
        functools.partial(apply_kernel, groups),
        out_shape=(
            jax.ShapeDtypeStruct((groups, BLOCK, LANES), BF16),
            jax.ShapeDtypeStruct((SIDE, PLANE), F32),
        ),
        in_specs=[HBM] * 6,
        out_specs=(HBM, VM),
        scratch_shapes=[
            box, box, box, box, slab, slab, slab,
            pltpu.VMEM((4 * PLANE, PLANE), BF16),
            pltpu.VMEM((PLANE, 3 * PLANE), BF16),
            side_lhs, side_lhs,
            pltpu.VMEM((side, 2 * side), BF16),
            pltpu.VMEM((CAP * groups, LANES), BF16),
            pltpu.VMEM((CAP * groups * CHUNKS, LANES), F32),
            pltpu.VMEM((groups, BLOCK, LANES), BF16),
            pltpu.VMEM((SIDE // 2, PLANE, 2 * LANES), BF16),
            pltpu.SMEM((SIDE,), F32), pltpu.SMEM((SIDE,), F32),
            pltpu.VMEM((1, LANES), F32), pltpu.VMEM((1, LANES), jnp.int32),
            dma, dma, dma, pltpu.SemaphoreType.DMA((CAP * 6,)),
        ],
        compiler_params=pltpu.CompilerParams(vmem_limit_bytes=48 * 1024 * 1024),
        name="apply",
    )(*[
        pltpu.with_memory_space_constraint(v, pltpu.HBM)
        for v in (magic_taps, kinetic_taps, kernel_diag.reshape(1, LANES), owners.reshape(1, LANES), support, potential)
    ])


def select_kernel(groups, owner_ref, out_ref):
    owner = owner_ref[...]
    column = slot_of(owner) * groups + owner
    down = jnp.broadcast_to(column.astype(F32), (LANES, LANES)).T
    lane = lax.broadcasted_iota(jnp.int32, (LANES, LANES), 1).astype(F32)
    for t in range(CAP * groups // LANES + 1):
        out_ref[:, t * LANES : (t + 1) * LANES] = jnp.where(down == lane + float(t * LANES), 1.0, 0.0).astype(BF16)


def run_select(owners, groups):
    return pl.pallas_call(
        functools.partial(select_kernel, groups),
        out_shape=jax.ShapeDtypeStruct((LANES, 2 * LANES), BF16),
        in_specs=[VM],
        out_specs=VM,
        name="select",
    )(owners.reshape(1, LANES))


def margin_kernel(groups, recv_ref, coef_ref, scale_ref, slab_ref, out_ref, rows_ref, back_ref):
    for g in range(groups):
        for s in range(CAP):
            block = recv_ref[g, s * CHUNKS : (s + 1) * CHUNKS, :].astype(F32)
            row = (s * (groups // 8) + g // 8) * (8 * CHUNKS) + g % 8 * 8
            for q in range(CHUNKS // 8):
                rows_ref[pl.ds(row + q * 64, 8), :] = block[q * 8 : q * 8 + 8]

    def column(c):
        start = c // 8 * 64 + c % 8
        tiles = [
            rows_ref[pl.ds(start + t * 8 * CHUNKS, 8, stride=8), :] for t in range(CAP * groups // 8)
        ]
        return jnp.concatenate(tiles, axis=0)

    acc = jnp.zeros((CAP * groups, LANES), F32)
    for i in range(SIDE):
        lhs = jnp.concatenate([column(2 * i), column(2 * i + 1)], axis=1).astype(BF16)
        acc = acc + mm(lhs, coef_ref[i * PLANE : (i + 1) * PLANE, :])
    acc = acc * (scale_ref[...] * (1.0 / float(SIDE) ** 1.5))
    for s in range(CAP):
        back_ref[pl.ds(s, groups, stride=BACK), :] = acc[s * groups : (s + 1) * groups]
    slab = slab_ref[...]
    for h in range(2):
        back_ref[pl.ds(CAP + h, groups, stride=BACK), :] = jnp.broadcast_to(
            slab[:, h * LANES : (h + 1) * LANES], (groups, LANES)
        )
    back_ref[pl.ds(CAP + 2, groups, stride=BACK), :] = jnp.zeros((groups, LANES), F32)
    out_ref[...] = back_ref[...].astype(BF16)


def run_margin(received, owned, kernel_diag, slab, groups):
    return pl.pallas_call(
        functools.partial(margin_kernel, groups),
        out_shape=jax.ShapeDtypeStruct((groups * BACK, LANES), BF16),
        in_specs=[VM, VM, VM, VM],
        out_specs=VM,
        scratch_shapes=[
            pltpu.VMEM((CAP * groups * CHUNKS, LANES), F32),
            pltpu.VMEM((groups * BACK, LANES), F32),
        ],
        compiler_params=pltpu.CompilerParams(vmem_limit_bytes=16 * 1024 * 1024),
        name="margin",
    )(received, owned, kernel_diag.reshape(1, LANES), slab)


def gather_kernel(groups, select_ref, ret_hbm, out_ref, dens_ref, ret_ref, back_ref, sem):
    copy = pltpu.make_async_copy(ret_hbm, ret_ref, sem)
    copy.start()
    copy.wait()
    back_ref[...] = ret_ref[...].astype(F32)
    rows = [back_ref[pl.ds(s, groups, stride=BACK), :] for s in range(CAP + 2)]
    x = jnp.concatenate(rows[:CAP] + [jnp.zeros((groups, LANES), F32)], axis=0)
    out_ref[...] = mm(select_ref[...], x.astype(BF16))
    for h in range(2):
        dens_ref[:, h * LANES : (h + 1) * LANES] = jnp.sum(
            rows[CAP + h].reshape(groups // HALF, HALF, LANES), axis=0
        )


def run_gather(select, returned, groups):
    return pl.pallas_call(
        functools.partial(gather_kernel, groups),
        out_shape=(
            jax.ShapeDtypeStruct((LANES, LANES), F32),
            jax.ShapeDtypeStruct((HALF, PLANE), F32),
        ),
        in_specs=[VM, HBM],
        out_specs=(VM, VM),
        scratch_shapes=[
            pltpu.VMEM((groups * BACK, LANES), BF16),
            pltpu.VMEM((groups * BACK, LANES), F32),
            pltpu.SemaphoreType.DMA,
        ],
        compiler_params=pltpu.CompilerParams(vmem_limit_bytes=4 * 1024 * 1024),
        name="gather",
    )(select, returned)


def body(support, potential, magic_taps, kinetic_taps, kernel_diag, owners):
    groups = lax.axis_size("grp")
    domains = lax.axis_size("dom")
    outgoing, part = run_apply(support, potential, magic_taps, kinetic_taps, kernel_diag, owners, groups)
    received = lax.all_to_all(outgoing, "grp", split_axis=0, concat_axis=0, tiled=True)
    owners_late, support_late, part = lax.optimization_barrier((owners, support, part))
    select = run_select(owners_late, groups)
    owned = support_late.reshape(CELLS, LANES).astype(BF16)
    distance = 1
    while distance < HALF:
        part = part + lax.ppermute(part, "grp", [(i, i ^ distance) for i in range(groups)])
        distance *= 2
    upper = lax.ppermute(part[HALF:], "dom", [(i, (i + 1) % domains) for i in range(domains)])
    mine = lax.axis_index("grp") % HALF
    slab = lax.dynamic_slice_in_dim(part[:HALF] + upper, mine, 1, 0)
    slab, select = lax.optimization_barrier((slab, select))
    products = run_margin(received, owned, kernel_diag, slab, groups)
    returned = lax.all_to_all(
        products.reshape(groups, BACK // 2, 2, LANES), "grp", split_axis=0, concat_axis=0, tiled=True
    )
    return run_gather(select, returned.reshape(groups * BACK, LANES), groups)


def solution(mesh):
    return jax.shard_map(
        body,
        mesh=mesh,
        in_specs=(
            P(None, None, None, ("dom", "grp")),
            P(None, None, None, ("dom", "grp")),
            P(),
            P(),
            P(("dom", "grp")),
            P(("dom", "grp"), None),
        ),
        out_specs=(P(("dom", "grp"), None), P("dom", None)),
        check_vma=False,
    )
```
